256 devices in a mesh: grp: 16 (over z, core), cls: 16 (over x, y).
Axes of the slice: x: 4, y: 4, z: 8, core: 2. Of those that a mesh axis runs over, the one named last changes fastest.
Arguments:
- particles: bfloat16 [4096, 16384], P(('grp', 'cls')), may hold values from -6 to 6
- candidates: int32 [4096, 8], P(('grp', 'cls')), may hold values from 0 to 207, all different within a row; in each aligned block of 16 rows (0 to 15, 16 to 31, ...) at most 2 rows name the same one
- group_ids: int32 [4096], P(('grp', 'cls')), may hold values from 0 to 63
- ctf_ids: int32 [4096], P(('grp', 'cls')), may hold values from 0 to 255
- ctf_table: float32 [256, 64], replicated, may hold values from -1 to 1
- noise_prec: float32 [64, 64], replicated, may hold values from 0.02 to 0.2
- references: bfloat16 [208, 16384], P('cls'), may hold values from -3 to 3
- log_prior: bfloat16 [208], P('cls'), may hold values from -4 to 4
- reg: float32 [64], replicated, may hold values from 0.1 to 1
Outputs:
- averages: float32 [208, 16384], P('cls')
- class_share: float32 [208], P('cls')
- log_mass: float32 [4096], P(('grp', 'cls'))
The draws below stay inside these ranges and needn't reach their ends.
Inputs may be any that keep to these rules, and one draw needn't show every extreme that they name: `candidates`: the 8 classes of a particle are distinct. Among the pairs of the rows of one device no class is named more than 2 times, a bound that some block reaches.
All inputs are finite; a program needn't handle non-finite values.
Results may differ from the reference program's by a relative error of at most 0.0046.
Values may be sent and summed in bfloat16 or wider, within the bound.
A program may use at most 128 MiB of HBM per device.

```python
import math
import jax
import jax.numpy as jnp
import numpy as np
from jax import lax

SHELLS = 64
FREQ = 128
FEAT = 16384
ROTS = 64
K = 208
CAND = 8
NGROUPS = 64
NCTF = 256
DEVICE_PARTICLES = 16
MOST = 2
PARTICLES = 4096
N_GRP = 16
N_CLS = 16


def draw_references(key, part):
    phase_key = jax.random.fold_in(key, 11)
    level_key = jax.random.fold_in(key, 12)
    base_key = jax.random.fold_in(key, 13)
    angle = jax.random.uniform(phase_key, (K, SHELLS, FREQ), jnp.float32, -math.pi, math.pi)
    base = jnp.exp(jax.random.uniform(base_key, (1, SHELLS, 1), jnp.float32, -0.5, 0.5))
    level = 1.0 + jax.random.uniform(level_key, (K, SHELLS, 1), jnp.float32, -0.1, 0.1)
    magnitude = base * jnp.sqrt(2.0 * level)
    real_part = magnitude * jnp.cos(angle)
    imag_part = magnitude * jnp.sin(angle)
    stacked = jnp.stack([real_part, imag_part], axis=1)
    return stacked.reshape(K, 2 * SHELLS * FREQ).astype(jnp.bfloat16)


def set_ends(array, stream_key, smallest, high):
    longest = array.shape.index(max(array.shape))
    spots = []
    for shift in (0, 1):
        where = [jax.random.randint(jax.random.fold_in(stream_key, axis), (), 0, length) for axis, length in enumerate(array.shape)]
        where[longest] = (where[longest] + shift) % array.shape[longest]
        spots.append(tuple(where))
    return array.at[spots[0]].set(smallest).at[spots[1]].set(high)


def steps_of(stream_key, dims, shards, least, high):
    def one(position, shards_of):
        draws = jax.random.uniform(jax.random.fold_in(jax.random.fold_in(stream_key, 6), position), (shards_of,), jnp.float32, least / len(shards), high / len(shards))
        return jnp.repeat(jnp.exp(draws), dims[position] // shards_of).reshape((-1,) + (1,) * (len(dims) - position - 1))

    loudness = one(*shards[0])
    for cut in shards[1:]:
        loudness = loudness * one(*cut)
    return loudness


def shared_out(own_key, own, number, rows, count, top, most, skew):
    order = jax.random.permutation(own_key, count)
    heavy_load, common = portions_of(count, rows * top, most, skew, True), portions_of(count, rows * top, most, skew, False)
    places = jnp.arange(count)

    def named(lengths, rotation):
        used = int((lengths > 0).sum())
        fixed = max(1, used // 4)
        moved = fixed + (places - fixed + rotation * (used - fixed)) % max(1, count - fixed)
        return jnp.zeros((count,), jnp.int32).at[order[jnp.where(places < fixed, places, moved)]].set(jnp.asarray(lengths, jnp.int32))

    lengths = jnp.where(number % 4 == 0, named(heavy_load, number // 4), named(common, number - number // 4 - 1))
    mixed = jax.random.permutation(jax.random.fold_in(own, 3), count)
    donor, sink = mixed[0:count // 2 * 2:2], mixed[1:count // 2 * 2:2]
    room = jnp.minimum(lengths[donor] - 1, most - lengths[sink]) // 2
    room = jnp.where((donor == order[0]) | (sink == order[0]) | (lengths[sink] == 0), 0, jnp.maximum(room, 0))
    moved = jax.random.randint(jax.random.fold_in(own, 4), (count // 2,), 0, 1 << 20) % (room + 1)
    lengths = lengths.at[donor].add(-moved).at[sink].add(moved)
    items = jnp.searchsorted(jnp.cumsum(lengths), jnp.arange(rows * top), side="right").astype(jnp.int32)
    grid = items.reshape(top, rows).T
    grid = grid[jax.random.permutation(jax.random.fold_in(own, 1), rows)]
    rotation = jax.random.randint(jax.random.fold_in(own, 2), (rows, 1), 0, top)
    return jnp.take_along_axis(grid, (jnp.arange(top)[None, :] + rotation) % top, axis=1)


def portions_of(count, total, reach, lean, full):
    portions = [(1 << 20) // math.isqrt(grade ** lean) + 1 for grade in range(1, count + 1)]
    largest = reach if full else min(reach, max(-(-total // count), total * portions[0] // sum(portions)))
    least = 1 if total - largest >= count - 1 else 0
    counts, spare = [largest] + [least] * (count - 1), total - largest - least * (count - 1)
    while spare > 0:
        movable = [i for i in range(1, count) if counts[i] < largest] or [i for i in range(1, count) if counts[i] < reach]
        mass, remaining = sum([portions[i] for i in movable]), spare
        for i in movable:
            more = min(reach - counts[i], max(1, remaining * portions[i] // mass), spare)
            counts[i] = counts[i] + more
            spare = spare - more
    return np.array(counts)


def scatter_about(rng, dims, spread, most, pieces=(), held_as=jnp.bfloat16):
    values = jax.random.normal(rng, dims, jnp.float32) * spread
    if len(pieces) > 0:
        values = steps_of(rng, dims, pieces, -0.22, 0.18) * values
    return jnp.clip(values, min=-most, max=most).astype(held_as)


def setup_inputs(seed: int = 0) -> dict:
    key_list = jax.random.split(jax.random.key(seed), 10)
    particles = scatter_about(key_list[0], (PARTICLES, FEAT), 1.0, 6.0, ((0, 256),))
    candidates_keys = jax.random.split(jax.random.fold_in(key_list[1], 1), PARTICLES // DEVICE_PARTICLES)
    candidates_turns = jax.random.permutation(jax.random.fold_in(key_list[1], 3), PARTICLES // DEVICE_PARTICLES)
    candidates = jax.vmap(lambda own, number: shared_out(jax.random.fold_in(key_list[1], 2), own, number, DEVICE_PARTICLES, K, CAND, MOST, 1))(candidates_keys, candidates_turns).reshape((PARTICLES, CAND))
    group_ids = set_ends(jax.random.randint(key_list[2], (PARTICLES,), 0, NGROUPS), jax.random.fold_in(key_list[2], 1), 0, NGROUPS - 1).astype(jnp.int32)
    ctf_ids = set_ends(jax.random.randint(key_list[3], (PARTICLES,), 0, NCTF), jax.random.fold_in(key_list[3], 1), 0, NCTF - 1).astype(jnp.int32)
    ctf_table = jnp.clip(jax.random.uniform(key_list[4], (NCTF, SHELLS), jnp.float32, -1.0, 1.0), -1.0, 1.0)
    noise_prec = jnp.clip(jnp.exp(jax.random.uniform(key_list[5], (NGROUPS, SHELLS), jnp.float32, math.log(0.02), math.log(0.2))), 0.02, 0.2)
    references = draw_references(jax.random.fold_in(key_list[9], 71), 0)
    log_prior = scatter_about(key_list[7], (K,), 1.0, 4.0, ((0, 16),))
    reg = jnp.clip(jnp.exp(jax.random.uniform(key_list[8], (SHELLS,), jnp.float32, math.log(0.1), math.log(1.0))), 0.1, 1.0)
    return dict(particles=particles, candidates=candidates, group_ids=group_ids, ctf_ids=ctf_ids, ctf_table=ctf_table, noise_prec=noise_prec, references=references, log_prior=log_prior, reg=reg)


def phase_tables():
    turns = jnp.arange(ROTS, dtype=jnp.int32)[:, None]
    orders = jnp.arange(FREQ, dtype=jnp.int32)[None, :]
    angles = ((turns * orders) % ROTS).astype(jnp.float32) * (2.0 * math.pi / ROTS)
    return jnp.cos(angles), jnp.sin(angles)


def cross_sums(rows, image):
    upper_limit = lax.Precision.HIGHEST
    count = rows.shape[0]
    particle_pieces = rows.astype(jnp.float32).reshape(count, 2, SHELLS, FREQ)
    image_components = image.astype(jnp.float32).reshape(2, SHELLS, FREQ)
    exchanged_rows = jnp.stack([image_components[1], -image_components[0]])
    inner_loop = jnp.einsum("kbqi,bqi->ki", particle_pieces, image_components, precision=upper_limit)
    outer_loop = jnp.einsum("kbqi,bqi->ki", particle_pieces, exchanged_rows, precision=upper_limit)
    return inner_loop, outer_loop


def rotation_scores(inner_loop, outer_loop, cos_tab, sin_tab):
    upper_limit = lax.Precision.HIGHEST
    return jnp.einsum("nf,jf->nj", inner_loop, cos_tab, precision=upper_limit) + jnp.einsum("nf,jf->nj", outer_loop, sin_tab, precision=upper_limit)


def reference(particles, candidates, group_ids, ctf_ids, ctf_table, noise_prec, references, log_prior, reg):
    cos_tab, sin_tab = phase_tables()
    pair_count = PARTICLES * CAND
    capacity = MOST * N_GRP * N_CLS
    precision_rows = noise_prec[group_ids]
    ctf_rows = ctf_table[ctf_ids]
    shell_weight = precision_rows * ctf_rows
    weighted = (particles.astype(jnp.float32).reshape(PARTICLES, 2, SHELLS, FREQ) * shell_weight[:, None, :, None]).reshape(PARTICLES, FEAT)
    weighted = lax.optimization_barrier(weighted.astype(jnp.bfloat16))
    shell_side = lax.optimization_barrier((precision_rows * ctf_rows * ctf_rows).astype(jnp.bfloat16))
    side_wide = shell_side.astype(jnp.float32)
    shell_power = jnp.sum(jnp.square(references.astype(jnp.float32)).reshape(K, 2, SHELLS, FREQ), axis=(1, 3))
    prior = log_prior.astype(jnp.float32)
    flat_class = candidates.reshape(pair_count).astype(jnp.int32)

    def members(class_index):
        found = jnp.nonzero(flat_class == class_index, size=capacity, fill_value=pair_count)[0].astype(jnp.int32)
        valid = found < pair_count
        clamped_values = jnp.minimum(found, pair_count - 1).astype(jnp.int32)
        return found, valid, clamped_values, clamped_values // CAND

    def score_class(carry, class_index):
        found, valid, clamped_values, row_index = members(class_index)
        picked = weighted[row_index]
        single = lax.dynamic_index_in_dim(references, class_index, 0, keepdims=False)
        inner_loop, outer_loop = cross_sums(picked, single)
        correlation = rotation_scores(inner_loop, outer_loop, cos_tab, sin_tab)
        penalty = jnp.sum(side_wide[row_index] * shell_power[class_index][None, :], axis=1)
        values = correlation - 0.5 * penalty[:, None] + prior[class_index]
        return carry.at[found].set(values, mode="drop"), None

    scores, unused = lax.scan(score_class, jnp.zeros((pair_count, ROTS), jnp.float32), jnp.arange(K, dtype=jnp.int32))
    scores = scores.reshape(PARTICLES, CAND * ROTS)
    best = jnp.max(scores, axis=1, keepdims=True)
    exponent = jnp.exp(scores - best)
    total_mass = jnp.sum(exponent, axis=1, keepdims=True)
    weights = lax.optimization_barrier((exponent / total_mass).astype(jnp.bfloat16))
    log_mass = jnp.log(total_mass[:, 0])
    pair_weights = weights.reshape(pair_count, ROTS).astype(jnp.float32)
    pair_sums = jnp.sum(pair_weights, axis=1)

    def gather_class(class_index):
        found, valid, clamped_values, row_index = members(class_index)
        chosen = jnp.where(valid[:, None], pair_weights[clamped_values], 0.0)
        wcos = lax.optimization_barrier(jnp.dot(chosen, cos_tab, precision=lax.Precision.HIGHEST).astype(jnp.bfloat16)).astype(jnp.float32)
        wsin = lax.optimization_barrier(jnp.dot(chosen, sin_tab, precision=lax.Precision.HIGHEST).astype(jnp.bfloat16)).astype(jnp.float32)
        particle_pieces = weighted[row_index].astype(jnp.float32).reshape(capacity, 2, SHELLS, FREQ)
        real_part = particle_pieces[:, 0]
        imag_part = particle_pieces[:, 1]
        upper_limit = lax.Precision.HIGHEST
        num_real = jnp.einsum("srf,sf->rf", real_part, wcos, precision=upper_limit) - jnp.einsum("srf,sf->rf", imag_part, wsin, precision=upper_limit)
        num_imag = jnp.einsum("srf,sf->rf", real_part, wsin, precision=upper_limit) + jnp.einsum("srf,sf->rf", imag_part, wcos, precision=upper_limit)
        numerator = jnp.stack([num_real, num_imag]).reshape(FEAT)
        sums = jnp.where(valid, pair_sums[clamped_values], 0.0)
        denominator = jnp.sum(sums[:, None] * side_wide[row_index], axis=0)
        return numerator, denominator, jnp.sum(sums)

    numerator, denominator, class_mass = lax.map(gather_class, jnp.arange(K, dtype=jnp.int32))
    divisor = denominator[:, None, :, None] + reg[None, None, :, None]
    averages = (numerator.reshape(K, 2, SHELLS, FREQ) / divisor).reshape(K, FEAT)
    class_share = class_mass * (K / PARTICLES)
    return averages, class_share, log_mass
```

```python
import math

import jax
import jax.numpy as jnp
import numpy as np
from jax import lax
from jax.experimental import pallas as pl
from jax.experimental.pallas import tpu as pltpu
from jax.sharding import PartitionSpec as P

SHELLS = 64
FREQ = 128
FEAT = 16384
ROTS = 64
K = 208
CAND = 8
OWN = 13
PART = 16
GROUP = 4
SL = SHELLS // GROUP
A_HALF = 7
B_HALF = OWN - A_HALF

MESH = pl.DeviceIdType.MESH
F32 = jnp.float32
BF16 = jnp.bfloat16
HIGH = lax.Precision.HIGHEST
VMEM = pltpu.VMEM


def np_tables():
    turns = np.arange(ROTS)[:, None]
    orders = np.arange(FREQ)[None, :]
    angles = (turns * orders % ROTS) * (2.0 * math.pi / ROTS)
    return np.cos(angles).astype(np.float32), np.sin(angles).astype(np.float32)


def score_tables():
    cos_tab, sin_tab = np_tables()
    both = np.concatenate([cos_tab.T, sin_tab.T], axis=0)
    out = np.zeros((2, 2 * FREQ, 2 * ROTS), np.float32)
    out[0, :, :ROTS] = both
    out[1, :, ROTS:] = both
    return out


def weight_tables():
    cos_tab, sin_tab = np_tables()
    both = np.concatenate([cos_tab, sin_tab], axis=1)
    out = np.zeros((2, 2 * ROTS, 2 * FREQ), np.float32)
    out[0, :ROTS] = both
    out[1, ROTS:] = both
    return out


def remote(src, dst, ssem, rsem, device):
    return pltpu.make_async_remote_copy(
        src_ref=src, dst_ref=dst, send_sem=ssem, recv_sem=rsem, device_id=device, device_id_type=MESH
    )


class Plane:
    def __init__(self):
        self.g = lax.axis_index("grp")
        self.c = lax.axis_index("cls")
        self.X = self.c // 4
        self.Y = self.c % 4

    def at(self, dx, dy):
        return ((self.X + dx) % 4) * 4 + (self.Y + dy) % 4


N_AG = 40


def score_kernel(
    cand_ref, crow_ref, w4_ref, refs4_ref, pwb_ref, side_ref, tab_ref,
    wall, wt_all, cand_all, lm_ref,
    refs_all, pw_all, cand_s, acc, sc_send, sc_recv, gmat,
    ag_send, ag_recv, pw_send, pw_recv, gw_send, gw_recv, gc_send, gc_recv,
    gs_send, gs_recv, gt_send, gt_recv, loc_sem,
):
    me = Plane()
    g, c = me.g, me.c
    q = g % GROUP
    base = g - q

    def member(d):
        return base + (q + d) % GROUP

    barrier = pltpu.get_barrier_semaphore()
    for d in range(1, 16):
        pl.semaphore_signal(barrier, inc=1, device_id=(g, (c + d) % 16), device_id_type=MESH)
    for d in range(1, GROUP):
        pl.semaphore_signal(barrier, inc=1, device_id=(member(d), c), device_id_type=MESH)
    pl.semaphore_wait(barrier, 18)

    def offs(h, i, j):
        return me.at(i, j) if h == 0 else me.at(j, i)

    def block(h, i, j, part):
        first = offs(h, i, j) * OWN
        if part == 0:
            return refs_all.at[h, pl.ds(first, OWN)]
        if part == 1:
            return refs_all.at[h, pl.ds(first, A_HALF)]
        return refs_all.at[h, pl.ds(first + A_HALF, B_HALF)]

    sends = []

    def send(m, src, dst, dev):
        cp = remote(src, dst, ag_send.at[m], ag_recv.at[m], (g, dev))
        cp.start()
        sends.append(cp)

    def arrived(m, dst):
        remote(dst, dst, ag_send.at[m], ag_recv.at[m], (g, c)).wait_recv()

    mine = [refs4_ref.at[q, h] for h in (0, 1)]
    where = (0, -1, 1, 2)

    def stage_two(h, n):
        i = where[n]
        src = mine[h] if n == 0 else block(h, i, 0, 0)
        m = h * 20 + 4 + 4 * n
        send(m, src, block(h, i, 0, 0), offs(h, 0, 1))
        send(m + 1, src, block(h, i, 0, 0), offs(h, 0, -1))

    def forward_two(h, n):
        i = where[n]
        m = h * 20 + 4 + 4 * n
        arrived(m, block(h, i, -1, 0))
        send(m + 2, block(h, i, -1, 1), block(h, i, -1, 1), offs(h, 0, 1))
        arrived(m + 1, block(h, i, 1, 0))
        send(m + 3, block(h, i, 1, 2), block(h, i, 1, 2), offs(h, 0, -1))

    for h in (0, 1):
        send(h * 20 + 0, mine[h], block(h, 0, 0, 0), offs(h, 1, 0))
        send(h * 20 + 1, mine[h], block(h, 0, 0, 0), offs(h, -1, 0))
        stage_two(h, 0)

    group_sends = []
    for d in range(1, GROUP):
        cp = remote(cand_ref, cand_all.at[q], gc_send.at[d], gc_recv.at[d], (member(d), c))
        cp.start()
        group_sends.append(cp)
        cp = remote(
            w4_ref.at[(q + d) % GROUP], wall.at[q], gw_send.at[d], gw_recv.at[d], (member(d), c)
        )
        cp.start()
        group_sends.append(cp)
    row0 = pl.multiple_of(c * 16, 16)
    for d in range(1, 16):
        cp = remote(
            pwb_ref, pw_all.at[pl.ds(row0, 16)], pw_send.at[d], pw_recv.at[d], (g, (c + d) % 16)
        )
        cp.start()
        group_sends.append(cp)
    local = [
        pltpu.make_async_copy(w4_ref.at[q], wall.at[q], loc_sem.at[0]),
        pltpu.make_async_copy(cand_ref, cand_all.at[q], loc_sem.at[1]),
        pltpu.make_async_copy(pwb_ref, pw_all.at[pl.ds(row0, 16)], loc_sem.at[2]),
        pltpu.make_async_copy(mine[0], block(0, 0, 0, 0), loc_sem.at[3]),
        pltpu.make_async_copy(mine[1], block(1, 0, 0, 0), loc_sem.at[4]),
    ]
    for cp in local:
        cp.start()

    for h in (0, 1):
        m = h * 20
        arrived(m, block(h, -1, 0, 0))
        send(m + 2, block(h, -1, 0, 1), block(h, -1, 0, 1), offs(h, 1, 0))
        stage_two(h, 1)
        arrived(m + 1, block(h, 1, 0, 0))
        send(m + 3, block(h, 1, 0, 2), block(h, 1, 0, 2), offs(h, -1, 0))
        stage_two(h, 2)
    for h in (0, 1):
        forward_two(h, 0)
    for h in (0, 1):
        arrived(h * 20 + 2, block(h, 2, 0, 1))
        arrived(h * 20 + 3, block(h, 2, 0, 2))
        stage_two(h, 3)
    for n in (1, 2, 3):
        for h in (0, 1):
            forward_two(h, n)

    for cp in local:
        cp.wait()
    for d in range(1, 16):
        rows = pw_all.at[pl.ds(pl.multiple_of((c - d + 16) % 16 * 16, 16), 16)]
        remote(rows, rows, pw_send.at[d], pw_recv.at[d], (g, c)).wait_recv()
    for d in range(1, GROUP):
        slot = cand_all.at[(q - d + GROUP) % GROUP]
        remote(slot, slot, gc_send.at[d], gc_recv.at[d], (g, c)).wait_recv()
    to_smem = pltpu.make_async_copy(cand_all, cand_s, loc_sem.at[5])
    to_smem.start()
    for i in range(PART):
        side_row = side_ref[i : i + 1, :]
        for t in range(CAND):
            gmat[i // 8, (i % 8) * 8 + t : (i % 8) * 8 + t + 1, :] = (
                side_row * pw_all[pl.ds(crow_ref[i * CAND + t], 1), :]
            )
    to_smem.wait()
    for d in range(1, GROUP):
        slot = wall.at[(q - d + GROUP) % GROUP]
        remote(slot, slot, gw_send.at[d], gw_recv.at[d], (g, c)).wait_recv()
    for h in (0, 1):
        for n in range(4):
            m = h * 20 + 4 + 4 * n
            arrived(m + 2, block(h, where[n], 2, 1))
            arrived(m + 3, block(h, where[n], 2, 2))

    @pl.loop(0, GROUP * PART)
    def _(n):
        s, i = n // PART, n % PART
        w_re = wall[s, i, 0].astype(F32)
        w_im = wall[s, i, 1].astype(F32)
        inner, outer = [], []
        for t in range(CAND):
            k = cand_s[s, 0, i * CAND + t]
            a_re = refs_all[0, k].astype(F32)
            a_im = refs_all[1, k].astype(F32)
            one = w_re * a_re + w_im * a_im
            two = w_re * a_im - w_im * a_re
            inner.append(jnp.sum(one, axis=0, keepdims=True))
            outer.append(jnp.sum(two, axis=0, keepdims=True))
        rows = pl.ds(pl.multiple_of(i % 8 * 8, 8), 8)
        acc[s, i // 8, rows, 0:FREQ] = jnp.concatenate(inner, axis=0)
        acc[s, i // 8, rows, FREQ : 2 * FREQ] = jnp.concatenate(outer, axis=0)

    @pl.loop(0, GROUP)
    def _(s):
        sc_send[s] = jnp.dot(
            acc[s, 0], tab_ref[0], precision=HIGH, preferred_element_type=F32
        ) + jnp.dot(acc[s, 1], tab_ref[1], precision=HIGH, preferred_element_type=F32)

    for d in range(1, GROUP):
        cp = remote(
            sc_send.at[(q + d) % GROUP], sc_recv.at[d], gs_send.at[d], gs_recv.at[d], (member(d), c)
        )
        cp.start()
        group_sends.append(cp)
    sc = sc_send[q]
    wide = lax.broadcasted_iota(jnp.int32, (64, 2 * ROTS), 1) < ROTS
    sc = sc + jnp.where(
        wide,
        jnp.sum(gmat[0], axis=1, keepdims=True),
        jnp.sum(gmat[1], axis=1, keepdims=True),
    )
    for d in range(1, GROUP):
        remote(sc_recv.at[d], sc_recv.at[d], gs_send.at[d], gs_recv.at[d], (g, c)).wait_recv()
    sc = sc + sc_recv[1] + sc_recv[2] + sc_recv[3]

    sc = sc.reshape(8, 8, 2 * ROTS)
    left = lax.broadcasted_iota(jnp.int32, (8, 2 * ROTS), 1) < ROTS
    low = jnp.max(sc, axis=1)
    best_l = jnp.max(jnp.where(left, low, -jnp.inf), axis=1, keepdims=True)
    best_r = jnp.max(jnp.where(left, -jnp.inf, low), axis=1, keepdims=True)
    best = jnp.where(left, best_l, best_r)
    expo = jnp.exp(sc - best[:, None, :])
    part = jnp.sum(expo, axis=1)
    tot_l = jnp.sum(jnp.where(left, part, 0.0), axis=1, keepdims=True)
    tot_r = jnp.sum(jnp.where(left, 0.0, part), axis=1, keepdims=True)
    total = jnp.where(left, tot_l, tot_r)
    lm_ref[...] = jnp.log(total)
    wt_all[q] = (expo / total[:, None, :]).reshape(64, 2 * ROTS).astype(BF16)
    for d in range(1, GROUP):
        cp = remote(
            wt_all.at[q], wt_all.at[q], gt_send.at[d], gt_recv.at[d], (member(d), c)
        )
        cp.start()
        group_sends.append(cp)
    for d in range(1, GROUP):
        slot = wt_all.at[(q - d + GROUP) % GROUP]
        remote(slot, slot, gt_send.at[d], gt_recv.at[d], (g, c)).wait_recv()
    for cp in sends + group_sends:
        cp.wait_send()


def sums_kernel(
    cand_s, krow_s, crow_s, wall, wt_all, wt_own, side_ref, tab_ref,
    num_ref, den_ref,
    acc, fac, psum,
):
    @pl.loop(0, 4 * OWN)
    def _(n):
        acc[:, pl.ds(n * 4, 4)] = jnp.zeros((2, 4, SL, FREQ), F32)

    den_ref[...] = jnp.zeros_like(den_ref)

    @pl.loop(0, GROUP)
    def _(s):
        wt = wt_all[s].astype(F32)
        for half in (0, 1):
            rows = jnp.dot(wt, tab_ref[half], precision=HIGH, preferred_element_type=F32)
            fac[s, half] = rows.astype(BF16).astype(F32)

    own = wt_own[...].astype(F32)
    lane = lax.broadcasted_iota(jnp.int32, own.shape, 1)
    psum[0] = jnp.broadcast_to(
        jnp.sum(jnp.where(lane < ROTS, own, 0.0), axis=1, keepdims=True), own.shape
    )
    psum[1] = jnp.broadcast_to(
        jnp.sum(jnp.where(lane < ROTS, 0.0, own), axis=1, keepdims=True), own.shape
    )

    @pl.loop(0, GROUP * PART)
    def _(n):
        s, i = n // PART, n % PART
        w_re = wall[s, i, 0].astype(F32)
        w_im = wall[s, i, 1].astype(F32)
        rows = pl.ds(pl.multiple_of(i % 8 * 8, 8), 8)
        cos8 = fac[s, i // 8, rows, 0:FREQ]
        sin8 = fac[s, i // 8, rows, FREQ : 2 * FREQ]
        for t in range(CAND):
            wcos, wsin = cos8[t : t + 1], sin8[t : t + 1]
            k0 = krow_s[n * CAND + t]
            k1 = cand_s[n * CAND + t]
            acc[0, k0] = acc[0, k0] + (w_re * wcos - w_im * wsin)
            acc[1, k1] = acc[1, k1] + (w_re * wsin + w_im * wcos)

    @pl.loop(0, PART)
    def _(i):
        side_row = side_ref[pl.ds(i, 1), :]
        sum8 = psum[i // 8, pl.ds(pl.multiple_of(i % 8 * 8, 8), 8), :]
        for t in range(CAND):
            row = pl.ds(crow_s[i * CAND + t], 1)
            den_ref[row, :] = den_ref[row, :] + side_row * sum8[t : t + 1]

    @pl.loop(0, 16)
    def _(o):
        for h in (0, 1):
            num_ref[h, o] = acc[h, pl.ds(o * OWN, OWN)].astype(BF16)


def reduce_kernel(
    num_ref, den_ref,
    fall, dtot_ref,
    rb1p, rb1m, rb2p, rb2m, sbp, sbm, rsum,
    qb1p, qb1m, qb2p, qb2m, tbp, tbm, tf, tz, zr, d1, d1r, d2r,
    s1s, s1r, zs, zrs, fs, fr, ss, sr, ds1, dr1, ds2, dr2,
):
    me = Plane()
    g, c = me.g, me.c
    barrier = pltpu.get_barrier_semaphore()
    for d in range(1, 16):
        pl.semaphore_signal(barrier, inc=1, device_id=(g, (c + d) % 16), device_id_type=MESH)
        pl.semaphore_signal(barrier, inc=1, device_id=((g + d) % 16, c), device_id_type=MESH)
    pl.semaphore_wait(barrier, 30)

    outgoing = []

    def go(src, dst, ssem, rsem, dev):
        cp = remote(src, dst, ssem, rsem, dev)
        cp.start()
        outgoing.append(cp)

    def got(dst, ssem, rsem):
        remote(dst, dst, ssem, rsem, (g, c)).wait_recv()

    def axis_dev(h, stage, delta):
        along_y = (h == 0) == (stage == 1)
        return (g, me.at(0, delta) if along_y else me.at(delta, 0))

    lo, hi = slice(0, A_HALF), slice(A_HALF, OWN)
    nsem = {}

    def sem(h, stage, name):
        key = (h, stage, name)
        if key not in nsem:
            nsem[key] = len(nsem)
        return s1s.at[nsem[key]], s1r.at[nsem[key]]

    first = (me.Y, me.X)
    second = (me.X, me.Y)

    for h in (0, 1):
        u = first[h]
        two = num_ref.at[h, (u + 2) % 4]
        go(two.at[:, lo], rb1p.at[h], *sem(h, 1, "1p"), axis_dev(h, 1, 1))
        go(two.at[:, hi], rb1m.at[h], *sem(h, 1, "1m"), axis_dev(h, 1, -1))
    for h in (0, 1):
        u = first[h]
        go(num_ref.at[h, (u + 1) % 4, :, hi], rb2p.at[h, :, hi], *sem(h, 1, "2pa"), axis_dev(h, 1, 1))
        go(num_ref.at[h, (u + 3) % 4, :, lo], rb2m.at[h, :, lo], *sem(h, 1, "2ma"), axis_dev(h, 1, -1))

    for d in range(1, 16):
        o = (c + d) % 16
        go(den_ref.at[pl.ds(pl.multiple_of(o * 16, 16), 16)], d1r.at[d], ds1.at[d], dr1.at[d], (g, o))

    for h in (0, 1):
        u = first[h]
        got(rb1p.at[h], *sem(h, 1, "1p"))
        for v in range(4):
            sbp[h, v] = (
                num_ref[h, (u + 1) % 4, v, lo].astype(F32) + rb1p[h, v].astype(F32)
            ).astype(BF16)
        go(sbp.at[h], rb2p.at[h, :, lo], *sem(h, 1, "2pb"), axis_dev(h, 1, 1))
        got(rb1m.at[h], *sem(h, 1, "1m"))
        for v in range(4):
            sbm[h, v] = (
                num_ref[h, (u + 3) % 4, v, hi].astype(F32) + rb1m[h, v].astype(F32)
            ).astype(BF16)
        go(sbm.at[h], rb2m.at[h, :, hi], *sem(h, 1, "2mb"), axis_dev(h, 1, -1))

    tot = den_ref[pl.ds(pl.multiple_of(c * 16, 16), 16), :]
    for d in range(1, 16):
        got(d1r.at[d], ds1.at[d], dr1.at[d])
        tot = tot + d1r[d]
    d1[...] = tot
    for d in range(1, 16):
        go(d1, d2r.at[d], ds2.at[d], dr2.at[d], ((g + d) % 16, c))

    for h in (0, 1):
        u, v0 = first[h], second[h]
        got(rb2p.at[h, :, hi], *sem(h, 1, "2pa"))
        got(rb2m.at[h, :, lo], *sem(h, 1, "2ma"))
        got(rb2p.at[h, :, lo], *sem(h, 1, "2pb"))
        got(rb2m.at[h, :, hi], *sem(h, 1, "2mb"))
        for j in (2, 1, 3, 0):
            v = (v0 + j) % 4
            val = num_ref[h, u, v].astype(F32) + rb2p[h, v].astype(F32) + rb2m[h, v].astype(F32)
            if j == 0:
                tf[h * OWN : (h + 1) * OWN] = val
            else:
                rsum[h, j] = val.astype(BF16)
            if j == 2:
                go(rsum.at[h, 2, lo], qb1p.at[h], *sem(h, 2, "1p"), axis_dev(h, 2, 1))
                go(rsum.at[h, 2, hi], qb1m.at[h], *sem(h, 2, "1m"), axis_dev(h, 2, -1))
            if j == 1:
                go(rsum.at[h, 1, hi], qb2p.at[h, hi], *sem(h, 2, "2pa"), axis_dev(h, 2, 1))
            if j == 3:
                go(rsum.at[h, 3, lo], qb2m.at[h, lo], *sem(h, 2, "2ma"), axis_dev(h, 2, -1))
    for h in (0, 1):
        got(qb1p.at[h], *sem(h, 2, "1p"))
        tbp[h] = (rsum[h, 1, lo].astype(F32) + qb1p[h].astype(F32)).astype(BF16)
        go(tbp.at[h], qb2p.at[h, lo], *sem(h, 2, "2pb"), axis_dev(h, 2, 1))
        got(qb1m.at[h], *sem(h, 2, "1m"))
        tbm[h] = (rsum[h, 3, hi].astype(F32) + qb1m[h].astype(F32)).astype(BF16)
        go(tbm.at[h], qb2m.at[h, hi], *sem(h, 2, "2mb"), axis_dev(h, 2, -1))
    tf[2 * OWN : 28] = jnp.zeros((28 - 2 * OWN, SL, FREQ), F32)
    for h in (0, 1):
        got(qb2p.at[h, hi], *sem(h, 2, "2pa"))
        got(qb2m.at[h, lo], *sem(h, 2, "2ma"))
        got(qb2p.at[h, lo], *sem(h, 2, "2pb"))
        got(qb2m.at[h, hi], *sem(h, 2, "2mb"))
        tf[h * OWN : (h + 1) * OWN] = (
            tf[h * OWN : (h + 1) * OWN] + qb2p[h].astype(F32) + qb2m[h].astype(F32)
        )
    tz[...] = tf[...].astype(BF16)

    for d in range(1, 4):
        peer = (g + 4 * d) % 16
        go(tz.at[pl.ds(peer // 4 * 7, 7)], zr.at[d], zs.at[d], zrs.at[d], (peer, c))
    for d in range(1, 16):
        got(d2r.at[d], ds2.at[d], dr2.at[d])
        tot = tot + d2r[d]
    dtot_ref[...] = tot
    val = tf[pl.ds(g // 4 * 7, 7)]
    for d in range(1, 4):
        got(zr.at[d], zs.at[d], zrs.at[d])
        val = val + zr[d].astype(F32)
    fall[g] = val.astype(BF16)

    sibling = g // 2 * 2 + (g + 1) % 2
    for d in (4, 3, 5, 2, 6, 1, 7):
        go(fall.at[g], fall.at[g], fs.at[d], fr.at[d], ((g + 2 * d) % 16, c))
    go(fall.at[g], fall.at[g], ss.at[0], sr.at[0], (sibling, c))
    for d in (1, 7, 2, 6, 3, 5, 4):
        src = fall.at[(g - 2 * d + 16) % 16]
        got(src, fs.at[d], fr.at[d])
        go(src, src, ss.at[d], sr.at[d], (sibling, c))
    for d in range(8):
        src = fall.at[(sibling - 2 * d + 16) % 16]
        got(src, ss.at[d], sr.at[d])
    for cp in outgoing:
        cp.wait_send()


def pair_scores(cand, crow, w4, refs4, pwb, side):
    dma = pltpu.SemaphoreType.DMA
    return pl.pallas_call(
        score_kernel,
        out_shape=(
            jax.ShapeDtypeStruct((GROUP, PART, 2, SL, FREQ), BF16),
            jax.ShapeDtypeStruct((GROUP, 64, 2 * ROTS), BF16),
            jax.ShapeDtypeStruct((GROUP, 8, 128), jnp.int32),
            jax.ShapeDtypeStruct((8, 128), F32),
        ),
        in_specs=[pl.BlockSpec(memory_space=VMEM), pl.BlockSpec(memory_space=pltpu.SMEM)]
        + [pl.BlockSpec(memory_space=VMEM)] * 5,
        out_specs=(pl.BlockSpec(memory_space=VMEM),) * 4,
        scratch_shapes=[
            VMEM((2, K, SL, FREQ), BF16),
            VMEM((256, 128), F32),
            pltpu.SMEM((GROUP, 8, 128), jnp.int32),
            VMEM((GROUP, 2, 64, 2 * FREQ), F32),
            VMEM((GROUP, 64, 2 * ROTS), F32),
            VMEM((GROUP, 64, 2 * ROTS), F32),
            VMEM((2, 64, 128), F32),
            dma((N_AG,)), dma((N_AG,)), dma((16,)), dma((16,)),
            dma((4,)), dma((4,)), dma((4,)), dma((4,)),
            dma((4,)), dma((4,)), dma((4,)), dma((4,)), dma((8,)),
        ],
        compiler_params=pltpu.CompilerParams(collective_id=0, has_side_effects=True),
        name="scores",
    )(cand, crow, w4, refs4, pwb, side, jnp.asarray(score_tables()))


def class_sums(cand, krow, crow, wall, wt_all, wt_own, side):
    return pl.pallas_call(
        sums_kernel,
        out_shape=(
            jax.ShapeDtypeStruct((2, 16, OWN, SL, FREQ), BF16),
            jax.ShapeDtypeStruct((256, 128), F32),
        ),
        in_specs=[pl.BlockSpec(memory_space=pltpu.SMEM)] * 3
        + [pl.BlockSpec(memory_space=VMEM)] * 5,
        out_specs=(pl.BlockSpec(memory_space=VMEM),) * 2,
        scratch_shapes=[
            VMEM((2, K, SL, FREQ), F32),
            VMEM((GROUP, 2, 64, 2 * FREQ), F32),
            VMEM((2, 64, 128), F32),
        ],
        name="sums",
    )(cand, krow, crow, wall, wt_all, wt_own, side, jnp.asarray(weight_tables()))


def reduce_all(num, den):
    dma = pltpu.SemaphoreType.DMA
    blk = (SL, FREQ)
    return pl.pallas_call(
        reduce_kernel,
        out_shape=(
            jax.ShapeDtypeStruct((16, 7) + blk, BF16),
            jax.ShapeDtypeStruct((16, 128), F32),
        ),
        in_specs=[pl.BlockSpec(memory_space=VMEM)] * 2,
        out_specs=(pl.BlockSpec(memory_space=VMEM),) * 2,
        scratch_shapes=[
            VMEM((2, 4, A_HALF) + blk, BF16), VMEM((2, 4, B_HALF) + blk, BF16),
            VMEM((2, 4, OWN) + blk, BF16), VMEM((2, 4, OWN) + blk, BF16),
            VMEM((2, 4, A_HALF) + blk, BF16), VMEM((2, 4, B_HALF) + blk, BF16),
            VMEM((2, 4, OWN) + blk, BF16),
            VMEM((2, A_HALF) + blk, BF16), VMEM((2, B_HALF) + blk, BF16),
            VMEM((2, OWN) + blk, BF16), VMEM((2, OWN) + blk, BF16),
            VMEM((2, A_HALF) + blk, BF16), VMEM((2, B_HALF) + blk, BF16),
            VMEM((28,) + blk, F32), VMEM((28,) + blk, BF16), VMEM((4, 7) + blk, BF16),
            VMEM((16, 128), F32), VMEM((16, 16, 128), F32), VMEM((16, 16, 128), F32),
            dma((24,)), dma((24,)), dma((4,)), dma((4,)), dma((8,)), dma((8,)), dma((8,)), dma((8,)),
            dma((16,)), dma((16,)), dma((16,)), dma((16,)),
        ],
        compiler_params=pltpu.CompilerParams(collective_id=1, has_side_effects=True),
        name="reduce",
    )(num, den)


def shell_terms(group_ids, ctf_ids, ctf_table, noise_prec):
    group_hot = (
        group_ids[:, None] == jnp.arange(noise_prec.shape[0], dtype=jnp.int32)[None, :]
    ).astype(F32)
    table_hot = (
        ctf_ids[:, None] == jnp.arange(ctf_table.shape[0], dtype=jnp.int32)[None, :]
    ).astype(F32)
    precision_rows = jnp.dot(group_hot, noise_prec, precision=HIGH)
    ctf_rows = jnp.dot(table_hot, ctf_table, precision=HIGH)
    weight = precision_rows * ctf_rows
    return weight, lax.reduce_precision(weight * ctf_rows, 8, 7)


def per_device(
    particles, candidates, group_ids, ctf_ids, ctf_table, noise_prec, references, log_prior, reg
):
    total = PART * lax.axis_size("grp") * lax.axis_size("cls")
    shell_weight, shell_side = shell_terms(group_ids, ctf_ids, ctf_table, noise_prec)
    w4 = (
        particles.astype(F32).reshape(PART, 2, GROUP, SL, FREQ)
        * shell_weight.reshape(PART, 1, GROUP, SL, 1)
    ).astype(BF16).transpose(2, 0, 1, 3, 4)
    refs4 = references.reshape(OWN, 2, GROUP, SL, FREQ).transpose(2, 1, 0, 3, 4)
    power = jnp.sum(
        jnp.square(references.astype(F32)).reshape(OWN, 2, SHELLS, FREQ), axis=(1, 3)
    )
    pwb = jnp.zeros((16, 128), F32)
    pwb = pwb.at[:OWN, :SHELLS].set(-0.5 * power).at[:OWN, SHELLS].set(log_prior.astype(F32))
    side = jnp.concatenate(
        [shell_side, jnp.ones((PART, 1), F32), jnp.zeros((PART, 63), F32)], axis=1
    )
    flat = candidates.reshape(PART * CAND)
    owner = flat // OWN
    inner = flat - owner * OWN
    crow = owner * 16 + inner
    krow = (owner % 4 * 4 + owner // 4) * OWN + inner
    cand = jnp.concatenate([flat[None], krow[None], jnp.zeros((6, 128), jnp.int32)], axis=0)

    wall, wt_all, cand_all, lm = pair_scores(cand, crow, w4, refs4, pwb, side)
    log_mass = jnp.concatenate([lm[:, 0], lm[:, ROTS]])
    own = lax.axis_index("grp") % GROUP
    wt_own = lax.dynamic_index_in_dim(wt_all, own, 0, keepdims=False)
    num, den = class_sums(
        cand_all[:, 0].reshape(-1), cand_all[:, 1].reshape(-1), crow, wall, wt_all, wt_own, side
    )
    fall, dtot = reduce_all(num.reshape(2, 4, 4, OWN, SL, FREQ), den)

    numerator = (
        fall.reshape(4, GROUP, 7, SL, FREQ)
        .transpose(0, 2, 1, 3, 4)
        .reshape(28, SHELLS, FREQ)[: 2 * OWN]
        .reshape(2, OWN, SHELLS, FREQ)
        .astype(F32)
    )
    divisor = dtot[:OWN, :SHELLS] + reg[None, :]
    averages = (numerator / divisor[None, :, :, None]).transpose(1, 0, 2, 3).reshape(OWN, FEAT)
    class_share = dtot[:OWN, SHELLS] * (K / total)
    return (averages, class_share, log_mass)


def solution(mesh):
    return jax.shard_map(
        per_device,
        mesh=mesh,
        in_specs=(
            P(("grp", "cls"), None),
            P(("grp", "cls"), None),
            P(("grp", "cls")),
            P(("grp", "cls")),
            P(),
            P(),
            P("cls", None),
            P("cls"),
            P(),
        ),
        out_specs=(P("cls", None), P("cls"), P(("grp", "cls"))),
        check_vma=False,
    )
```

```python
import functools
import math

import jax
import jax.numpy as jnp
import numpy as np
from jax import lax
from jax.experimental import pallas as pl
from jax.experimental.pallas import tpu as pltpu
from jax.sharding import PartitionSpec as P

SHELLS = 64
FREQ = 128
FEAT = 16384
ROTS = 64
K = 208
CAND = 8
OWN = 13
PART = 16
GROUP = 4
SL = SHELLS // GROUP
A_HALF = 7
B_HALF = OWN - A_HALF

MESH = pl.DeviceIdType.MESH
F32 = jnp.float32
BF16 = jnp.bfloat16
HIGH = lax.Precision.HIGHEST
VMEM = pltpu.VMEM


def np_tables():
    turns = np.arange(ROTS)[:, None]
    orders = np.arange(FREQ)[None, :]
    angles = (turns * orders % ROTS) * (2.0 * math.pi / ROTS)
    return np.cos(angles).astype(np.float32), np.sin(angles).astype(np.float32)


def score_tables():
    cos_tab, sin_tab = np_tables()
    both = np.concatenate([cos_tab.T, sin_tab.T], axis=0)
    out = np.zeros((2, 2 * FREQ, 2 * ROTS), np.float32)
    out[0, :, :ROTS] = both
    out[1, :, ROTS:] = both
    return out


def weight_tables():
    cos_tab, sin_tab = np_tables()
    both = np.concatenate([cos_tab, sin_tab], axis=1)
    out = np.zeros((2, 2 * ROTS, 2 * FREQ), np.float32)
    out[0, :ROTS] = both
    out[1, ROTS:] = both
    return out


def remote(src, dst, ssem, rsem, device):
    return pltpu.make_async_remote_copy(
        src_ref=src, dst_ref=dst, send_sem=ssem, recv_sem=rsem, device_id=device, device_id_type=MESH
    )


def split(value):
    high = value.astype(BF16)
    left = lax.broadcasted_iota(jnp.int32, value.shape, len(value.shape) - 1) < ROTS
    return jnp.where(left, high.astype(F32), value - high.astype(F32)).astype(BF16)


def whole(pair):
    wide = pair.astype(F32)
    return wide + pltpu.roll(wide, ROTS, axis=1)


class Plane:
    def __init__(self):
        self.g = lax.axis_index("grp")
        self.c = lax.axis_index("cls")
        self.X = self.c // 4
        self.Y = self.c % 4

    def at(self, dx, dy):
        return ((self.X + dx) % 4) * 4 + (self.Y + dy) % 4


N_AG = 40


SIZE = (OWN + 1, OWN)
BLANK = GROUP * PART * CAND


def em_kernel(
    cand_ref, cand_sm, slot_ref, w4_ref, refs4_ref, pwb_ref, side_ref, tab_ref, wtab_ref,
    fall, lm_ref,
    wall, wt_all, cand_all, side_all, slot_all,
    refs_all, pw_all, cand_s, slot_s, acc, sc_send, sc_recv, gmat,
    wf, wcos, wsin, drow, den,
    num0, rb1p0, rb1m0, rb2p0, rb2m0, sbp0, sbm0, rsum0, qr0,
    num1, rb1p1, rb1m1, rb2p1, rb2m1, sbp1, sbm1, rsum1, qr1,
    tf, tz, zr,
    ag_send, ag_recv, pw_send, pw_recv, gw_send, gw_recv, gc_send, gc_recv,
    gs_send, gs_recv, gt_send, gt_recv, gd_send, gd_recv, gl_send, gl_recv, loc_sem,
    s1s, s1r, zs, zrs, fs, fr, ss, sr,
):
    me = Plane()
    g, c = me.g, me.c
    q = g % GROUP
    base = g - q

    def member(d):
        return base + (q + d) % GROUP

    sibling = g // 2 * 2 + (g + 1) % 2
    barrier = pltpu.get_barrier_semaphore()
    for d in range(1, 16):
        pl.semaphore_signal(barrier, inc=1, device_id=(g, (c + d) % 16), device_id_type=MESH)
        pl.semaphore_signal(barrier, inc=1, device_id=((g + d) % 16, c), device_id_type=MESH)
    pl.semaphore_wait(barrier, 30)

    def offs(h, i, j):
        return me.at(i, j) if h == 0 else me.at(j, i)

    def block(h, i, j, part):
        first = offs(h, i, j) * OWN
        if part == 0:
            return refs_all.at[h, pl.ds(first, OWN)]
        if part == 1:
            return refs_all.at[h, pl.ds(first, A_HALF)]
        return refs_all.at[h, pl.ds(first + A_HALF, B_HALF)]

    sends = []

    def send(m, src, dst, dev):
        cp = remote(src, dst, ag_send.at[m], ag_recv.at[m], (g, dev))
        cp.start()
        sends.append(cp)

    def arrived(m, dst):
        remote(dst, dst, ag_send.at[m], ag_recv.at[m], (g, c)).wait_recv()

    mine = [refs4_ref.at[q, h] for h in (0, 1)]
    where = (0, -1, 1, 2)

    def stage_two(h, n):
        i = where[n]
        src = mine[h] if n == 0 else block(h, i, 0, 0)
        m = h * 20 + 4 + 4 * n
        send(m, src, block(h, i, 0, 0), offs(h, 0, 1))
        send(m + 1, src, block(h, i, 0, 0), offs(h, 0, -1))

    def forward_two(h, n):
        i = where[n]
        m = h * 20 + 4 + 4 * n
        arrived(m, block(h, i, -1, 0))
        send(m + 2, block(h, i, -1, 1), block(h, i, -1, 1), offs(h, 0, 1))
        arrived(m + 1, block(h, i, 1, 0))
        send(m + 3, block(h, i, 1, 2), block(h, i, 1, 2), offs(h, 0, -1))

    for h in (0, 1):
        send(h * 20 + 0, mine[h], block(h, 0, 0, 0), offs(h, 1, 0))
        send(h * 20 + 1, mine[h], block(h, 0, 0, 0), offs(h, -1, 0))
        stage_two(h, 0)

    group_sends = []
    for d in range(1, GROUP):
        cp = remote(cand_ref, cand_all.at[q], gc_send.at[d], gc_recv.at[d], (member(d), c))
        cp.start()
        group_sends.append(cp)
        cp = remote(slot_ref, slot_all.at[q], gl_send.at[d], gl_recv.at[d], (member(d), c))
        cp.start()
        group_sends.append(cp)
        cp = remote(side_ref, side_all.at[q], gd_send.at[d], gd_recv.at[d], (member(d), c))
        cp.start()
        group_sends.append(cp)
        cp = remote(
            w4_ref.at[(q + d) % GROUP], wall.at[q], gw_send.at[d], gw_recv.at[d], (member(d), c)
        )
        cp.start()
        group_sends.append(cp)
    row0 = pl.multiple_of(c * 16, 16)
    for d in range(1, 16):
        cp = remote(
            pwb_ref, pw_all.at[pl.ds(row0, 16)], pw_send.at[d], pw_recv.at[d], (g, (c + d) % 16)
        )
        cp.start()
        group_sends.append(cp)
    local = [
        pltpu.make_async_copy(w4_ref.at[q], wall.at[q], loc_sem.at[0]),
        pltpu.make_async_copy(cand_ref, cand_all.at[q], loc_sem.at[1]),
        pltpu.make_async_copy(pwb_ref, pw_all.at[pl.ds(row0, 16)], loc_sem.at[2]),
        pltpu.make_async_copy(mine[0], block(0, 0, 0, 0), loc_sem.at[3]),
        pltpu.make_async_copy(mine[1], block(1, 0, 0, 0), loc_sem.at[4]),
        pltpu.make_async_copy(side_ref, side_all.at[q], loc_sem.at[6]),
        pltpu.make_async_copy(slot_ref, slot_all.at[q], loc_sem.at[7]),
    ]
    for cp in local:
        cp.start()

    for h in (0, 1):
        m = h * 20
        arrived(m, block(h, -1, 0, 0))
        send(m + 2, block(h, -1, 0, 1), block(h, -1, 0, 1), offs(h, 1, 0))
        stage_two(h, 1)
        arrived(m + 1, block(h, 1, 0, 0))
        send(m + 3, block(h, 1, 0, 2), block(h, 1, 0, 2), offs(h, -1, 0))
        stage_two(h, 2)
    for h in (0, 1):
        forward_two(h, 0)
    for h in (0, 1):
        arrived(h * 20 + 2, block(h, 2, 0, 1))
        arrived(h * 20 + 3, block(h, 2, 0, 2))
        stage_two(h, 3)
    for n in (1, 2, 3):
        for h in (0, 1):
            forward_two(h, n)

    for cp in local:
        cp.wait()
    for d in range(1, 16):
        rows = pw_all.at[pl.ds(pl.multiple_of((c - d + 16) % 16 * 16, 16), 16)]
        remote(rows, rows, pw_send.at[d], pw_recv.at[d], (g, c)).wait_recv()
    for d in range(1, GROUP):
        slot = cand_all.at[(q - d + GROUP) % GROUP]
        remote(slot, slot, gc_send.at[d], gc_recv.at[d], (g, c)).wait_recv()
    for d in range(1, GROUP):
        slot = slot_all.at[(q - d + GROUP) % GROUP]
        remote(slot, slot, gl_send.at[d], gl_recv.at[d], (g, c)).wait_recv()
    to_smem = pltpu.make_async_copy(cand_all, cand_s, loc_sem.at[5])
    to_smem.start()
    slots_to_smem = pltpu.make_async_copy(slot_all, slot_s, loc_sem.at[8])
    slots_to_smem.start()
    for i in range(PART):
        side_row = side_ref[i : i + 1, :]
        for t in range(CAND):
            k = cand_sm[t, i]
            gmat[i // 8, (i % 8) * 8 + t : (i % 8) * 8 + t + 1, :] = (
                side_row * pw_all[pl.ds(k // OWN * 16 + k % OWN, 1), :]
            )
    to_smem.wait()
    slots_to_smem.wait()
    for d in range(1, GROUP):
        slot = side_all.at[(q - d + GROUP) % GROUP]
        remote(slot, slot, gd_send.at[d], gd_recv.at[d], (g, c)).wait_recv()
        slot = wall.at[(q - d + GROUP) % GROUP]
        remote(slot, slot, gw_send.at[d], gw_recv.at[d], (g, c)).wait_recv()

    @pl.loop(0, GROUP * PART)
    def _(n):
        wf[n] = wall[n // PART, n % PART].astype(F32)

    wf[GROUP * PART] = jnp.zeros((2, SL, FREQ), F32)
    for h in (0, 1):
        for n in range(4):
            m = h * 20 + 4 + 4 * n
            arrived(m + 2, block(h, where[n], 2, 1))
            arrived(m + 3, block(h, where[n], 2, 2))

    @pl.loop(0, GROUP * PART)
    def _(n):
        s, i = n // PART, n % PART
        w_re, w_im = wf[n, 0], wf[n, 1]
        inner, outer = [], []
        for t in range(CAND):
            k = cand_s[s, t, i]
            a_re = refs_all[0, k].astype(F32)
            a_im = refs_all[1, k].astype(F32)
            one = w_re * a_re + w_im * a_im
            two = w_re * a_im - w_im * a_re
            inner.append(jnp.sum(one, axis=0, keepdims=True))
            outer.append(jnp.sum(two, axis=0, keepdims=True))
        rows = pl.ds(pl.multiple_of(i % 8 * 8, 8), 8)
        acc[s, i // 8, rows, 0:FREQ] = jnp.concatenate(inner, axis=0)
        acc[s, i // 8, rows, FREQ : 2 * FREQ] = jnp.concatenate(outer, axis=0)

    @pl.loop(0, GROUP)
    def _(s):
        sc_send[s] = jnp.dot(
            acc[s, 0], tab_ref[0], precision=HIGH, preferred_element_type=F32
        ) + jnp.dot(acc[s, 1], tab_ref[1], precision=HIGH, preferred_element_type=F32)

    for d in range(1, GROUP):
        cp = remote(
            sc_send.at[(q + d) % GROUP], sc_recv.at[d], gs_send.at[d], gs_recv.at[d], (member(d), c)
        )
        cp.start()
        group_sends.append(cp)
    sc = sc_send[q]
    wide = lax.broadcasted_iota(jnp.int32, (64, 2 * ROTS), 1) < ROTS
    sc = sc + jnp.where(
        wide,
        jnp.sum(gmat[0], axis=1, keepdims=True),
        jnp.sum(gmat[1], axis=1, keepdims=True),
    )
    for d in range(1, GROUP):
        remote(sc_recv.at[d], sc_recv.at[d], gs_send.at[d], gs_recv.at[d], (g, c)).wait_recv()
    sc = sc + sc_recv[1] + sc_recv[2] + sc_recv[3]

    sc = sc.reshape(8, 8, 2 * ROTS)
    left = lax.broadcasted_iota(jnp.int32, (8, 2 * ROTS), 1) < ROTS
    low = jnp.max(sc, axis=1)
    best_l = jnp.max(jnp.where(left, low, -jnp.inf), axis=1, keepdims=True)
    best_r = jnp.max(jnp.where(left, -jnp.inf, low), axis=1, keepdims=True)
    best = jnp.where(left, best_l, best_r)
    expo = jnp.exp(sc - best[:, None, :])
    part = jnp.sum(expo, axis=1)
    tot_l = jnp.sum(jnp.where(left, part, 0.0), axis=1, keepdims=True)
    tot_r = jnp.sum(jnp.where(left, 0.0, part), axis=1, keepdims=True)
    total = jnp.where(left, tot_l, tot_r)
    spot = lax.broadcasted_iota(jnp.int32, (8, 2 * ROTS), 1)
    particle = lax.broadcasted_iota(jnp.int32, (8, 2 * ROTS), 0)
    mass = jnp.where(spot == particle, tot_l, jnp.where(spot == particle + 8, tot_r, 0.0))
    lm_ref[...] = jnp.log(jnp.sum(mass, axis=0, keepdims=True)[:, :PART])
    wt_all[q] = (expo / total[:, None, :]).reshape(64, 2 * ROTS).astype(BF16)
    for d in range(1, GROUP):
        cp = remote(
            wt_all.at[q], wt_all.at[q], gt_send.at[d], gt_recv.at[d], (member(d), c)
        )
        cp.start()
        group_sends.append(cp)
    for d in range(1, GROUP):
        slot = wt_all.at[(q - d + GROUP) % GROUP]
        remote(slot, slot, gt_send.at[d], gt_recv.at[d], (g, c)).wait_recv()

    lane = lax.broadcasted_iota(jnp.int32, (64, 128), 1)
    for s in range(GROUP):
        wt = wt_all[s].astype(F32)
        for half in (0, 1):
            rows = jnp.dot(wt, wtab_ref[half], precision=HIGH, preferred_element_type=F32)
            rows = rows.astype(BF16).astype(F32)
            first = s * PART * CAND + half * 64
            wcos[first : first + 64] = rows[:, :FREQ]
            wsin[first : first + 64] = rows[:, FREQ:]
            part = jnp.where((lane < ROTS) == (half == 0), wt, 0.0)
            mass = jnp.sum(part, axis=1, keepdims=True)
            for i in range(8):
                drow[first + i * 8 : first + i * 8 + 8] = (
                    mass[i * 8 : i * 8 + 8] * side_all[s, half * 8 + i : half * 8 + i + 1, :]
                )
    for ref in (wcos, wsin, drow):
        ref[BLANK : BLANK + 8] = jnp.zeros((8, 128), F32)

    num = (num0, num1)
    small = lax.broadcasted_iota(jnp.int32, (16, 128), 1)

    def owner_sums(x, y):
        o = x * 4 + y

        @pl.loop(0, OWN)
        def _(kk):
            re = jnp.zeros((SL, FREQ), F32)
            im = jnp.zeros((SL, FREQ), F32)
            dd = jnp.zeros((1, 128), F32)
            for s in range(GROUP):
                for m in range(2):
                    row = slot_s[s, o, kk * 2 + m]
                    p = row >> 3
                    w_re, w_im = wf[p, 0], wf[p, 1]
                    wc, ws = wcos[pl.ds(row, 1), :], wsin[pl.ds(row, 1), :]
                    re = re + (w_re * wc - w_im * ws)
                    im = im + (w_re * ws + w_im * wc)
                    dd = dd + drow[pl.ds(row, 1), :]
            num0[y, x, kk] = re.astype(BF16)
            num1[x, y, kk] = im.astype(BF16)
            den[pl.ds(kk, 1), :] = dd

        rows = den[...]
        mine = pltpu.roll(rows, (128 - q * SL) % 128, axis=1)
        both = jnp.where(small < SL, mine, pltpu.roll(mine, ROTS, axis=1))
        num0[y, x, OWN] = split(jnp.where(small % ROTS < SL, both, rows[:, ROTS : ROTS + 1]))

    den[...] = jnp.zeros_like(den)

    rb1p, rb1m, rb2p, rb2m = (rb1p0, rb1p1), (rb1m0, rb1m1), (rb2p0, rb2p1), (rb2m0, rb2m1)
    sbp, sbm, rsum, qr = (sbp0, sbp1), (sbm0, sbm1), (rsum0, rsum1), (qr0, qr1)
    outgoing = []

    def go(src, dst, ssem, rsem, dev):
        cp = remote(src, dst, ssem, rsem, dev)
        cp.start()
        outgoing.append(cp)

    def got(dst, ssem, rsem):
        remote(dst, dst, ssem, rsem, (g, c)).wait_recv()

    def axis_dev(h, stage, delta):
        along_y = (h == 0) == (stage == 1)
        return (g, me.at(0, delta) if along_y else me.at(delta, 0))

    lo, hi = slice(0, A_HALF), (slice(A_HALF, SIZE[0]), slice(A_HALF, SIZE[1]))
    nsem = {}

    def sem(h, stage, name):
        key = (h, stage, name)
        if key not in nsem:
            nsem[key] = len(nsem)
        return s1s.at[nsem[key]], s1r.at[nsem[key]]

    def add_high(h, left, right):
        plain = (left[: OWN - A_HALF].astype(F32) + right[: OWN - A_HALF].astype(F32)).astype(BF16)
        if h == 1:
            return plain
        last = split(whole(left[OWN - A_HALF]) + whole(right[OWN - A_HALF]))
        return jnp.concatenate([plain, last[None]], axis=0)

    first = (me.Y, me.X)
    second = (me.X, me.Y)

    def first_sends(h):
        two = num[h].at[(first[h] + 2) % 4]
        go(two.at[:, lo], rb1p[h], *sem(h, 1, "1p"), axis_dev(h, 1, 1))
        go(two.at[:, hi[h]], rb1m[h], *sem(h, 1, "1m"), axis_dev(h, 1, -1))

    def plus_sends(h):
        u = (first[h] + 1) % 4
        go(num[h].at[u, :, hi[h]], rb2p[h].at[:, hi[h]], *sem(h, 1, "2pa"), axis_dev(h, 1, 1))

    def minus_sends(h):
        u = (first[h] + 3) % 4
        go(num[h].at[u, :, lo], rb2m[h].at[:, lo], *sem(h, 1, "2ma"), axis_dev(h, 1, -1))

    def plus_sum(h):
        got(rb1p[h], *sem(h, 1, "1p"))
        for v in range(4):
            sbp[h][v] = (
                num[h][(first[h] + 1) % 4, v, lo].astype(F32) + rb1p[h][v].astype(F32)
            ).astype(BF16)
        go(sbp[h], rb2p[h].at[:, lo], *sem(h, 1, "2pb"), axis_dev(h, 1, 1))

    def minus_sum(h):
        got(rb1m[h], *sem(h, 1, "1m"))
        for v in range(4):
            sbm[h][v] = add_high(h, num[h][(first[h] + 3) % 4, v, hi[h]], rb1m[h][v])
        go(sbm[h], rb2m[h].at[:, hi[h]], *sem(h, 1, "2mb"), axis_dev(h, 1, -1))

    X, Y = me.X, me.Y

    @pl.loop(0, 4)
    def _(n):
        owner_sums((X + 2 + n) % 4, (Y + 2) % 4)

    first_sends(0)

    @pl.loop(0, 3)
    def _(n):
        owner_sums((X + 2) % 4, (Y + 3 + n) % 4)

    first_sends(1)

    @pl.loop(0, 3)
    def _(n):
        owner_sums((X + 3 + n) % 4, (Y + 1) % 4)

    plus_sends(0)
    plus_sum(0)

    @pl.loop(0, 3)
    def _(n):
        owner_sums((X + 3 + n) % 4, (Y + 3) % 4)

    minus_sends(0)
    minus_sum(0)

    @pl.loop(0, 3)
    def _(n):
        owner_sums((X + 3 + n) % 4, Y)

    plus_sends(1)
    minus_sends(1)
    plus_sum(1)
    minus_sum(1)

    for h in (0, 1):
        u, v0 = first[h], second[h]
        got(rb2p[h].at[:, hi[h]], *sem(h, 1, "2pa"))
        got(rb2m[h].at[:, lo], *sem(h, 1, "2ma"))
        got(rb2p[h].at[:, lo], *sem(h, 1, "2pb"))
        got(rb2m[h].at[:, hi[h]], *sem(h, 1, "2mb"))
        for j in (2, 1, 3, 0):
            v = (v0 + j) % 4
            val = (
                num[h][u, v, 0:OWN].astype(F32)
                + rb2p[h][v, 0:OWN].astype(F32)
                + rb2m[h][v, 0:OWN].astype(F32)
            )
            if h == 0:
                tiny = whole(num[h][u, v, OWN]) + whole(rb2p[h][v, OWN]) + whole(rb2m[h][v, OWN])
            if j == 0:
                tf[h * OWN : (h + 1) * OWN] = val
                if h == 0:
                    tf[2 * OWN] = tiny
                continue
            rsum[h][j, 0:OWN] = val.astype(BF16)
            if h == 0:
                rsum[h][j, OWN] = split(tiny)
            go(rsum[h].at[j], qr[h].at[j], *sem(h, 2, str(j)), axis_dev(h, 2, j))
    for h in (0, 1):
        for j in (1, 3, 2):
            got(qr[h].at[j], *sem(h, 2, str(j)))
        tf[h * OWN : (h + 1) * OWN] = (
            tf[h * OWN : (h + 1) * OWN]
            + qr[h][1, 0:OWN].astype(F32)
            + qr[h][2, 0:OWN].astype(F32)
            + qr[h][3, 0:OWN].astype(F32)
        )
    tf[2 * OWN] = tf[2 * OWN] + whole(qr0[1, OWN]) + whole(qr0[2, OWN]) + whole(qr0[3, OWN])
    tf[2 * OWN + 1] = jnp.zeros((SL, FREQ), F32)
    tz[...] = tf[...].astype(BF16)
    tz[2 * OWN] = split(tf[2 * OWN])

    for d in (2, 1, 3):
        peer = (g + 4 * d) % 16
        go(tz.at[pl.ds(peer // 4 * 7, 7)], zr.at[d], zs.at[d], zrs.at[d], (peer, c))
    val = tf[pl.ds(g // 4 * 7, 7)]
    tiny = tf[2 * OWN]
    for d in (1, 3, 2):
        got(zr.at[d], zs.at[d], zrs.at[d])
        val = val + zr[d].astype(F32)
        tiny = tiny + whole(zr[d, 5])
    fall[g, 0:5] = val[0:5].astype(BF16)
    fall[g, 6] = val[6].astype(BF16)
    fall[g, 5] = jnp.where(g // 4 == 3, split(tiny), val[5].astype(BF16))

    for d in (4, 3, 5, 2, 6, 1, 7):
        go(fall.at[g], fall.at[g], fs.at[d], fr.at[d], ((g + 2 * d) % 16, c))
    go(fall.at[g], fall.at[g], ss.at[0], sr.at[0], (sibling, c))
    for d in (1, 7, 2, 6, 3, 5, 4):
        src = fall.at[(g - 2 * d + 16) % 16]
        got(src, fs.at[d], fr.at[d])
        go(src, src, ss.at[d], sr.at[d], (sibling, c))
    for d in range(8):
        src = fall.at[(sibling - 2 * d + 16) % 16]
        got(src, ss.at[d], sr.at[d])
    for cp in sends + group_sends + outgoing:
        cp.wait_send()


def finish_kernel(fall, reg_s, avg_ref, share_ref, wide, *, scale):
    small = [whole(fall[12 + s, 5]) for s in range(GROUP)]
    lane = lax.broadcasted_iota(jnp.int32, (16, 128), 1)
    row = lax.broadcasted_iota(jnp.int32, (16, 128), 0)
    mass = jnp.sum(jnp.where(lane == row, small[0][:, SL : SL + 1], 0.0), axis=0, keepdims=True)
    share_ref[...] = mass[:, :OWN] * scale
    for s in range(GROUP):
        for n in range(4):
            wide[s, pl.ds(n * 7 * SL, 7 * SL), :] = fall[n * 4 + s].astype(F32).reshape(7 * SL, FREQ)
    for s in range(GROUP):
        for r in range(SL):
            shell = s * SL + r
            inverse = 1.0 / (small[s][:OWN, r : r + 1] + reg_s[shell])
            for x in (0, 1):
                rows = wide[s, pl.ds(x * OWN * SL + r, OWN, stride=SL), :]
                first = (x * SHELLS + shell) * FREQ
                avg_ref[:, first : first + FREQ] = rows * inverse


VM = pl.BlockSpec(memory_space=VMEM)
SM = pl.BlockSpec(memory_space=pltpu.SMEM)


def em_sums(cand, slots, w4, refs4, pwb, side):
    dma = pltpu.SemaphoreType.DMA
    blk = (SL, FREQ)
    parts = []
    for n in SIZE:
        rest = n - A_HALF
        parts += [
            VMEM((4, 4, n) + blk, BF16),
            VMEM((4, A_HALF) + blk, BF16), VMEM((4, rest) + blk, BF16),
            VMEM((4, n) + blk, BF16), VMEM((4, n) + blk, BF16),
            VMEM((4, A_HALF) + blk, BF16), VMEM((4, rest) + blk, BF16),
            VMEM((4, n) + blk, BF16), VMEM((4, n) + blk, BF16),
        ]
    return pl.pallas_call(
        em_kernel,
        out_shape=(
            jax.ShapeDtypeStruct((16, 7) + blk, BF16),
            jax.ShapeDtypeStruct((1, PART), F32),
        ),
        in_specs=[VM, SM] + [VM] * 7,
        out_specs=(VM,) * 2,
        scratch_shapes=[
            VMEM((GROUP, PART, 2, SL, FREQ), BF16),
            VMEM((GROUP, 64, 2 * ROTS), BF16),
            VMEM((GROUP, CAND, PART), jnp.int32),
            VMEM((GROUP, PART, 128), F32),
            VMEM((GROUP, 16, 128), jnp.int32),
            VMEM((2, K, SL, FREQ), BF16),
            VMEM((256, 128), F32),
            pltpu.SMEM((GROUP, CAND, PART), jnp.int32),
            pltpu.SMEM((GROUP, 16, 128), jnp.int32),
            VMEM((GROUP, 2, 64, 2 * FREQ), F32),
            VMEM((GROUP, 64, 2 * ROTS), F32),
            VMEM((GROUP, 64, 2 * ROTS), F32),
            VMEM((2, 64, 128), F32),
            VMEM((GROUP * PART + 1, 2) + blk, F32),
            VMEM((BLANK + 8, 128), F32), VMEM((BLANK + 8, 128), F32), VMEM((BLANK + 8, 128), F32),
            VMEM((16, 128), F32),
        ] + parts + [
            VMEM((28,) + blk, F32), VMEM((28,) + blk, BF16), VMEM((4, 7) + blk, BF16),
            dma((N_AG,)), dma((N_AG,)), dma((16,)), dma((16,)),
            dma((4,)), dma((4,)), dma((4,)), dma((4,)),
            dma((4,)), dma((4,)), dma((4,)), dma((4,)),
            dma((4,)), dma((4,)), dma((4,)), dma((4,)), dma((9,)),
            dma((24,)), dma((24,)), dma((4,)), dma((4,)), dma((8,)), dma((8,)), dma((8,)), dma((8,)),
        ],
        compiler_params=pltpu.CompilerParams(collective_id=0, has_side_effects=True),
        name="em",
    )(
        cand, cand, slots, w4, refs4, pwb, side,
        jnp.asarray(score_tables()), jnp.asarray(weight_tables()),
    )


def slot_rows(candidates, group_member):
    flat = candidates.reshape(PART * CAND)
    pair = jnp.arange(PART * CAND, dtype=jnp.int32)
    same = flat[:, None] == flat[None, :]
    rank = jnp.sum((same & (pair[None, :] < pair[:, None])).astype(jnp.int32), axis=1)
    at = (flat * 2 + rank)[None, :] == jnp.arange(K * 2, dtype=jnp.int32)[:, None]
    found = jnp.sum(jnp.where(at, pair[None, :] + 1, 0), axis=1)
    row = jnp.where(found > 0, found - 1 + group_member * (PART * CAND), BLANK)
    return jnp.pad(row.reshape(16, 2 * OWN), ((0, 0), (0, 128 - 2 * OWN)))


def finish(fall, reg, scale):
    return pl.pallas_call(
        functools.partial(finish_kernel, scale=scale),
        out_shape=(
            jax.ShapeDtypeStruct((OWN, FEAT), F32),
            jax.ShapeDtypeStruct((1, OWN), F32),
        ),
        in_specs=[VM, SM],
        out_specs=(VM, VM),
        scratch_shapes=[VMEM((GROUP, 28 * SL, FREQ), F32)],
        name="finish",
    )(fall, reg)


def shell_terms(group_ids, ctf_ids, ctf_table, noise_prec):
    group_hot = (
        group_ids[:, None] == jnp.arange(noise_prec.shape[0], dtype=jnp.int32)[None, :]
    ).astype(F32)
    table_hot = (
        ctf_ids[:, None] == jnp.arange(ctf_table.shape[0], dtype=jnp.int32)[None, :]
    ).astype(F32)
    precision_rows = jnp.dot(group_hot, noise_prec, precision=HIGH)
    ctf_rows = jnp.dot(table_hot, ctf_table, precision=HIGH)
    weight = precision_rows * ctf_rows
    return weight, lax.reduce_precision(weight * ctf_rows, 8, 7)


def per_device(
    particles, candidates, group_ids, ctf_ids, ctf_table, noise_prec, references, log_prior, reg
):
    total = PART * lax.axis_size("grp") * lax.axis_size("cls")
    shell_weight, shell_side = shell_terms(group_ids, ctf_ids, ctf_table, noise_prec)
    w4 = (
        particles.astype(F32).reshape(PART, 2, GROUP, SL, FREQ)
        * shell_weight.reshape(PART, 1, GROUP, SL, 1)
    ).astype(BF16).transpose(2, 0, 1, 3, 4)
    refs4 = references.reshape(OWN, 2, GROUP, SL, FREQ).transpose(2, 1, 0, 3, 4)
    power = jnp.sum(
        jnp.square(references.astype(F32)).reshape(OWN, 2, SHELLS, FREQ), axis=(1, 3)
    )
    pwb = jnp.pad(
        jnp.concatenate([-0.5 * power, log_prior.astype(F32)[:, None]], axis=1),
        ((0, 16 - OWN), (0, 127 - SHELLS)),
    )
    side = jnp.pad(shell_side, ((0, 0), (0, 128 - SHELLS)), constant_values=1.0)
    slots = slot_rows(candidates, lax.axis_index("grp") % GROUP)
    fall, lm = em_sums(candidates.T, slots, w4, refs4, pwb, side)
    averages, share = finish(fall, reg, K / total)
    return (averages, share.reshape(OWN), lm.reshape(PART))


def solution(mesh):
    return jax.shard_map(
        per_device,
        mesh=mesh,
        in_specs=(
            P(("grp", "cls"), None),
            P(("grp", "cls"), None),
            P(("grp", "cls")),
            P(("grp", "cls")),
            P(),
            P(),
            P("cls", None),
            P("cls"),
            P(),
        ),
        out_specs=(P("cls", None), P("cls"), P(("grp", "cls"))),
        check_vma=False,
    )
```

```python
import functools
import math

import jax
import jax.numpy as jnp
import numpy as np
from jax import lax
from jax.experimental import pallas as pl
from jax.experimental.pallas import tpu as pltpu
from jax.sharding import PartitionSpec as P

SHELLS = 64
FREQ = 128
FEAT = 16384
ROTS = 64
K = 208
CAND = 8
OWN = 13
PART = 16
GROUP = 4
SL = SHELLS // GROUP
A_HALF = 7
B_HALF = OWN - A_HALF

MESH = pl.DeviceIdType.MESH
F32 = jnp.float32
BF16 = jnp.bfloat16
HIGH = lax.Precision.HIGHEST
VMEM = pltpu.VMEM


def np_tables():
    turns = np.arange(ROTS)[:, None]
    orders = np.arange(FREQ)[None, :]
    angles = (turns * orders % ROTS) * (2.0 * math.pi / ROTS)
    return np.cos(angles).astype(np.float32), np.sin(angles).astype(np.float32)


def score_tables():
    cos_tab, sin_tab = np_tables()
    both = np.concatenate([cos_tab.T, sin_tab.T], axis=0)
    out = np.zeros((2, 2 * FREQ, 2 * ROTS), np.float32)
    out[0, :, :ROTS] = both
    out[1, :, ROTS:] = both
    return out


def weight_tables():
    cos_tab, sin_tab = np_tables()
    both = np.concatenate([cos_tab, sin_tab], axis=1)
    out = np.zeros((2, 2 * ROTS, 2 * FREQ), np.float32)
    out[0, :ROTS] = both
    out[1, ROTS:] = both
    return out


def remote(src, dst, ssem, rsem, device):
    return pltpu.make_async_remote_copy(
        src_ref=src, dst_ref=dst, send_sem=ssem, recv_sem=rsem, device_id=device, device_id_type=MESH
    )


def split(value):
    high = value.astype(BF16)
    left = lax.broadcasted_iota(jnp.int32, value.shape, len(value.shape) - 1) < ROTS
    return jnp.where(left, high.astype(F32), value - high.astype(F32)).astype(BF16)


def whole(pair):
    wide = pair.astype(F32)
    return wide + pltpu.roll(wide, ROTS, axis=1)


class Plane:
    def __init__(self):
        self.g = lax.axis_index("grp")
        self.c = lax.axis_index("cls")
        self.X = self.c // 4
        self.Y = self.c % 4

    def at(self, dx, dy):
        return ((self.X + dx) % 4) * 4 + (self.Y + dy) % 4


N_AG = 40


SIZE = (OWN + 1, OWN)
BLANK = GROUP * PART * CAND


def em_kernel(
    part_hbm, refs_hbm, cand_ref, cand_sm, gid_sm, cid_sm, prior_sm, noise_ref, ctf_ref, tab_ref, wtab_ref,
    fall, lm_ref,
    part_ref, own_ref, spread, spread_refs, slot_ref, w4_ref, pwb_ref, side_ref,
    wall, wt_all, cand_all, side_all, slot_all,
    refs_all, pw_all, cand_s, slot_s, acc, sc_send, sc_recv, gmat,
    wf, fac, den,
    num0, rb1p0, rb1m0, rb2p0, rb2m0, sbp0, sbm0, rsum0, qr0,
    num1, rb1p1, rb1m1, rb2p1, rb2m1, sbp1, sbm1, rsum1, qr1,
    tf, tz, zr,
    ag_send, ag_recv, pw_send, pw_recv, gw_send, gw_recv, gc_send, gc_recv,
    gs_send, gs_recv, gt_send, gt_recv, gd_send, gd_recv, gl_send, gl_recv, loc_sem,
    s1s, s1r, zs, zrs, fs, fr, ss, sr,
):
    me = Plane()
    g, c = me.g, me.c
    q = g % GROUP
    base = g - q

    def member(d):
        return base + (q + d) % GROUP

    sibling = g // 2 * 2 + (g + 1) % 2
    barrier = pltpu.get_barrier_semaphore()
    for d in range(1, 16):
        pl.semaphore_signal(barrier, inc=1, device_id=(g, (c + d) % 16), device_id_type=MESH)
        pl.semaphore_signal(barrier, inc=1, device_id=((g + d) % 16, c), device_id_type=MESH)
    load_refs = pltpu.make_async_copy(refs_hbm, own_ref, loc_sem.at[3])
    load_refs.start()
    load_part = pltpu.make_async_copy(part_hbm, part_ref, loc_sem.at[4])
    load_part.start()

    lane16 = lax.broadcasted_iota(jnp.int32, (16, 128), 1)
    row16 = lax.broadcasted_iota(jnp.int32, (16, 128), 0)

    place = jnp.where(lane16 < 2 * OWN, row16 * (2 * OWN) + lane16, -1)
    last = jnp.full((16, 128), BLANK, jnp.int32)
    head = jnp.full((16, 128), BLANK, jnp.int32)
    for n in range(PART * CAND):
        low = place == 2 * cand_sm[n % CAND, n // CAND]
        last = jnp.where(low, q * (PART * CAND) + n, last)
        m = PART * CAND - 1 - n
        high = place == 2 * cand_sm[m % CAND, m // CAND]
        head = jnp.where(high, q * (PART * CAND) + m, head)
    other = jnp.where(head == last, BLANK, head)
    slot_ref[...] = jnp.where(lane16 % 2 == 0, last, pltpu.roll(other, 1, axis=1))

    def picked(ids, table, rows_are_lanes):
        count = table.shape[1] if rows_are_lanes else table.shape[0]
        spot = lax.broadcasted_iota(jnp.int32, (PART, count), 1)
        which = lax.broadcasted_iota(jnp.int32, (PART, count), 0)
        wanted = jnp.zeros((PART, count), jnp.int32)
        for i in range(PART):
            wanted = jnp.where(which == i, ids[i], wanted)
        hot = (wanted == spot).astype(F32).astype(BF16)
        dims = (((1,), (1 if rows_are_lanes else 0,)), ((), ()))
        rest, rows = table, jnp.zeros((PART, SHELLS), F32)
        for _ in range(3):
            piece = rest.astype(BF16)
            rest = rest - piece.astype(F32)
            rows = rows + lax.dot_general(hot, piece, dims, preferred_element_type=F32)
        return rows

    precision_rows = picked(gid_sm, noise_ref[...], False)
    ctf_rows = picked(cid_sm, ctf_ref[...], True)
    shell_weight = precision_rows * ctf_rows
    side_ref[:, SHELLS:] = jnp.ones((PART, 128 - SHELLS), F32)
    side_ref[:, :SHELLS] = (shell_weight * ctf_rows).astype(BF16).astype(F32)

    load_refs.wait()
    for x in (0, 1):
        for r in range(SL):
            first = pl.multiple_of((x * SHELLS + q * SL + r) * FREQ, FREQ)
            spread_refs[x, pl.ds(r, OWN, stride=SL), :] = own_ref[:, pl.ds(first, FREQ)].astype(F32)
        refs_all[x, pl.ds(c * OWN, OWN)] = (
            spread_refs[x].reshape(OWN, SL, FREQ).astype(BF16)
        )
    table = jnp.zeros((OWN, 128), F32)
    lane13 = lax.broadcasted_iota(jnp.int32, (OWN, 128), 1)
    row13 = lax.broadcasted_iota(jnp.int32, (OWN, 128), 0)
    for r in range(SHELLS):
        re = own_ref[:, r * FREQ : (r + 1) * FREQ].astype(F32)
        im = own_ref[:, (SHELLS + r) * FREQ : (SHELLS + r + 1) * FREQ].astype(F32)
        power = jnp.sum(re * re + im * im, axis=1, keepdims=True)
        table = jnp.where(lane13 == r, -0.5 * power, table)
    for k in range(OWN):
        table = jnp.where((lane13 == SHELLS) & (row13 == k), prior_sm[k], table)
    pwb_ref[...] = jnp.zeros((16, 128), F32)
    pwb_ref[0:OWN] = table

    load_part.wait()
    for s in range(GROUP):
        for r in range(SL):
            shell = s * SL + r
            column = shell_weight[:, shell : shell + 1]
            for x in (0, 1):
                first = (x * SHELLS + shell) * FREQ
                spread[s, x, pl.ds(r, PART, stride=SL), :] = (
                    part_ref[:, first : first + FREQ].astype(F32) * column
                )
        for x in (0, 1):
            w4_ref[s, :, x] = spread[s, x].reshape(PART, SL, FREQ).astype(BF16)

    pl.semaphore_wait(barrier, 30)

    def offs(h, i, j):
        return me.at(i, j) if h == 0 else me.at(j, i)

    def block(h, i, j, part):
        first = offs(h, i, j) * OWN
        if part == 0:
            return refs_all.at[h, pl.ds(first, OWN)]
        if part == 1:
            return refs_all.at[h, pl.ds(first, A_HALF)]
        return refs_all.at[h, pl.ds(first + A_HALF, B_HALF)]

    sends = []

    def send(m, src, dst, dev):
        cp = remote(src, dst, ag_send.at[m], ag_recv.at[m], (g, dev))
        cp.start()
        sends.append(cp)

    def arrived(m, dst):
        remote(dst, dst, ag_send.at[m], ag_recv.at[m], (g, c)).wait_recv()

    mine = [block(h, 0, 0, 0) for h in (0, 1)]
    where = (0, -1, 1, 2)

    def stage_two(h, n):
        i = where[n]
        src = mine[h] if n == 0 else block(h, i, 0, 0)
        m = h * 20 + 4 + 4 * n
        send(m, src, block(h, i, 0, 0), offs(h, 0, 1))
        send(m + 1, src, block(h, i, 0, 0), offs(h, 0, -1))

    def forward_two(h, n):
        i = where[n]
        m = h * 20 + 4 + 4 * n
        arrived(m, block(h, i, -1, 0))
        send(m + 2, block(h, i, -1, 1), block(h, i, -1, 1), offs(h, 0, 1))
        arrived(m + 1, block(h, i, 1, 0))
        send(m + 3, block(h, i, 1, 2), block(h, i, 1, 2), offs(h, 0, -1))

    for h in (0, 1):
        send(h * 20 + 0, mine[h], block(h, 0, 0, 0), offs(h, 1, 0))
        send(h * 20 + 1, mine[h], block(h, 0, 0, 0), offs(h, -1, 0))
    for h in (0, 1):
        stage_two(h, 0)

    group_sends = []
    for d in range(1, GROUP):
        cp = remote(cand_ref, cand_all.at[q], gc_send.at[d], gc_recv.at[d], (member(d), c))
        cp.start()
        group_sends.append(cp)
        cp = remote(slot_ref, slot_all.at[q], gl_send.at[d], gl_recv.at[d], (member(d), c))
        cp.start()
        group_sends.append(cp)
        cp = remote(side_ref, side_all.at[q], gd_send.at[d], gd_recv.at[d], (member(d), c))
        cp.start()
        group_sends.append(cp)
        cp = remote(
            w4_ref.at[(q + d) % GROUP], wall.at[q], gw_send.at[d], gw_recv.at[d], (member(d), c)
        )
        cp.start()
        group_sends.append(cp)
    row0 = pl.multiple_of(c * 16, 16)
    for d in range(1, 16):
        cp = remote(
            pwb_ref, pw_all.at[pl.ds(row0, 16)], pw_send.at[d], pw_recv.at[d], (g, (c + d) % 16)
        )
        cp.start()
        group_sends.append(cp)
    local = [
        pltpu.make_async_copy(w4_ref.at[q], wall.at[q], loc_sem.at[0]),
        pltpu.make_async_copy(cand_ref, cand_all.at[q], loc_sem.at[1]),
        pltpu.make_async_copy(pwb_ref, pw_all.at[pl.ds(row0, 16)], loc_sem.at[2]),
        pltpu.make_async_copy(side_ref, side_all.at[q], loc_sem.at[6]),
        pltpu.make_async_copy(slot_ref, slot_all.at[q], loc_sem.at[7]),
    ]
    for cp in local:
        cp.start()

    for h in (0, 1):
        m = h * 20
        arrived(m, block(h, -1, 0, 0))
        send(m + 2, block(h, -1, 0, 1), block(h, -1, 0, 1), offs(h, 1, 0))
        stage_two(h, 1)
        arrived(m + 1, block(h, 1, 0, 0))
        send(m + 3, block(h, 1, 0, 2), block(h, 1, 0, 2), offs(h, -1, 0))
        stage_two(h, 2)
    for h in (0, 1):
        forward_two(h, 0)
    for h in (0, 1):
        arrived(h * 20 + 2, block(h, 2, 0, 1))
        arrived(h * 20 + 3, block(h, 2, 0, 2))
        stage_two(h, 3)
    for n in (1, 2, 3):
        for h in (0, 1):
            forward_two(h, n)

    for cp in local:
        cp.wait()
    for d in range(1, 16):
        rows = pw_all.at[pl.ds(pl.multiple_of((c - d + 16) % 16 * 16, 16), 16)]
        remote(rows, rows, pw_send.at[d], pw_recv.at[d], (g, c)).wait_recv()
    for d in range(1, GROUP):
        slot = cand_all.at[(q - d + GROUP) % GROUP]
        remote(slot, slot, gc_send.at[d], gc_recv.at[d], (g, c)).wait_recv()
    for d in range(1, GROUP):
        slot = slot_all.at[(q - d + GROUP) % GROUP]
        remote(slot, slot, gl_send.at[d], gl_recv.at[d], (g, c)).wait_recv()
    to_smem = pltpu.make_async_copy(cand_all, cand_s, loc_sem.at[5])
    to_smem.start()
    slots_to_smem = pltpu.make_async_copy(slot_all, slot_s, loc_sem.at[8])
    slots_to_smem.start()
    for i in range(PART):
        side_row = side_ref[i : i + 1, :]
        for t in range(CAND):
            k = cand_sm[t, i]
            gmat[i // 8, (i % 8) * 8 + t : (i % 8) * 8 + t + 1, :] = (
                side_row * pw_all[pl.ds(k // OWN * 16 + k % OWN, 1), :]
            )
    to_smem.wait()
    slots_to_smem.wait()
    for d in range(1, GROUP):
        slot = side_all.at[(q - d + GROUP) % GROUP]
        remote(slot, slot, gd_send.at[d], gd_recv.at[d], (g, c)).wait_recv()
        slot = wall.at[(q - d + GROUP) % GROUP]
        remote(slot, slot, gw_send.at[d], gw_recv.at[d], (g, c)).wait_recv()

    @pl.loop(0, GROUP * PART)
    def _(n):
        wf[n] = wall[n // PART, n % PART].astype(F32)

    wf[GROUP * PART] = jnp.zeros((2, SL, FREQ), F32)
    for h in (0, 1):
        for n in range(4):
            m = h * 20 + 4 + 4 * n
            arrived(m + 2, block(h, where[n], 2, 1))
            arrived(m + 3, block(h, where[n], 2, 2))

    @pl.loop(0, GROUP * PART)
    def _(n):
        s, i = n // PART, n % PART
        w_re, w_im = wf[n, 0], wf[n, 1]
        inner, outer = [], []
        for t in range(CAND):
            k = cand_s[s, t, i]
            a_re = refs_all[0, k].astype(F32)
            a_im = refs_all[1, k].astype(F32)
            one = w_re * a_re + w_im * a_im
            two = w_re * a_im - w_im * a_re
            inner.append(jnp.sum(one, axis=0, keepdims=True))
            outer.append(jnp.sum(two, axis=0, keepdims=True))
        rows = pl.ds(pl.multiple_of(i % 8 * 8, 8), 8)
        acc[s, i // 8, rows, 0:FREQ] = jnp.concatenate(inner, axis=0)
        acc[s, i // 8, rows, FREQ : 2 * FREQ] = jnp.concatenate(outer, axis=0)

    @pl.loop(0, GROUP)
    def _(s):
        sc_send[s] = jnp.dot(
            acc[s, 0], tab_ref[0], precision=HIGH, preferred_element_type=F32
        ) + jnp.dot(acc[s, 1], tab_ref[1], precision=HIGH, preferred_element_type=F32)

    for d in range(1, GROUP):
        cp = remote(
            sc_send.at[(q + d) % GROUP], sc_recv.at[d], gs_send.at[d], gs_recv.at[d], (member(d), c)
        )
        cp.start()
        group_sends.append(cp)
    sc = sc_send[q]
    wide = lax.broadcasted_iota(jnp.int32, (64, 2 * ROTS), 1) < ROTS
    sc = sc + jnp.where(
        wide,
        jnp.sum(gmat[0], axis=1, keepdims=True),
        jnp.sum(gmat[1], axis=1, keepdims=True),
    )
    for d in range(1, GROUP):
        remote(sc_recv.at[d], sc_recv.at[d], gs_send.at[d], gs_recv.at[d], (g, c)).wait_recv()
    sc = sc + sc_recv[1] + sc_recv[2] + sc_recv[3]

    sc = sc.reshape(8, 8, 2 * ROTS)
    left = lax.broadcasted_iota(jnp.int32, (8, 2 * ROTS), 1) < ROTS
    low = jnp.max(sc, axis=1)
    best_l = jnp.max(jnp.where(left, low, -jnp.inf), axis=1, keepdims=True)
    best_r = jnp.max(jnp.where(left, -jnp.inf, low), axis=1, keepdims=True)
    best = jnp.where(left, best_l, best_r)
    expo = jnp.exp(sc - best[:, None, :])
    part = jnp.sum(expo, axis=1)
    tot_l = jnp.sum(jnp.where(left, part, 0.0), axis=1, keepdims=True)
    tot_r = jnp.sum(jnp.where(left, 0.0, part), axis=1, keepdims=True)
    total = jnp.where(left, tot_l, tot_r)
    spot = lax.broadcasted_iota(jnp.int32, (8, 2 * ROTS), 1)
    particle = lax.broadcasted_iota(jnp.int32, (8, 2 * ROTS), 0)
    mass = jnp.where(spot == particle, tot_l, jnp.where(spot == particle + 8, tot_r, 0.0))
    lm_ref[...] = jnp.log(jnp.sum(mass, axis=0, keepdims=True)[:, :PART])
    wt_all[q] = (expo / total[:, None, :]).reshape(64, 2 * ROTS).astype(BF16)
    for d in range(1, GROUP):
        cp = remote(
            wt_all.at[q], wt_all.at[q], gt_send.at[d], gt_recv.at[d], (member(d), c)
        )
        cp.start()
        group_sends.append(cp)
    for d in range(1, GROUP):
        slot = wt_all.at[(q - d + GROUP) % GROUP]
        remote(slot, slot, gt_send.at[d], gt_recv.at[d], (g, c)).wait_recv()

    lane = lax.broadcasted_iota(jnp.int32, (64, 128), 1)
    for s in range(GROUP):
        wt = wt_all[s].astype(F32)
        for half in (0, 1):
            rows = jnp.dot(wt, wtab_ref[half], precision=HIGH, preferred_element_type=F32)
            rows = rows.astype(BF16).astype(F32)
            first = s * PART * CAND + half * 64
            for n in range(64):
                fac[first + n, 0:8] = jnp.broadcast_to(rows[n : n + 1, :FREQ], (8, FREQ))
                fac[first + n, 8:16] = jnp.broadcast_to(rows[n : n + 1, FREQ:], (8, FREQ))
            part = jnp.where((lane < ROTS) == (half == 0), wt, 0.0)
            mass = jnp.sum(part, axis=1, keepdims=True)
            for i in range(8):
                terms = mass[i * 8 : i * 8 + 8] * side_all[s, half * 8 + i : half * 8 + i + 1, :]
                for t in range(CAND):
                    fac[first + i * 8 + t, 16:24] = jnp.broadcast_to(terms[t : t + 1], (8, 128))
    fac[BLANK] = jnp.zeros((24, 128), F32)

    num = (num0, num1)
    small = lax.broadcasted_iota(jnp.int32, (16, 128), 1)

    def owner_sums(x, y):
        o = x * 4 + y

        @pl.loop(0, OWN)
        def _(kk):
            re = [jnp.zeros((8, FREQ), F32)] * 2
            im = [jnp.zeros((8, FREQ), F32)] * 2
            dd = jnp.zeros((8, 128), F32)
            for s in range(GROUP):
                for m in range(2):
                    row = slot_s[s, o, kk * 2 + m]
                    p = row >> 3
                    wc, ws = fac[row, 0:8], fac[row, 8:16]
                    for n in (0, 1):
                        w_re, w_im = wf[p, 0, n * 8 : n * 8 + 8], wf[p, 1, n * 8 : n * 8 + 8]
                        re[n] = re[n] + (w_re * wc - w_im * ws)
                        im[n] = im[n] + (w_re * ws + w_im * wc)
                    dd = dd + fac[row, 16:24]
            re, im, dd = jnp.concatenate(re, axis=0), jnp.concatenate(im, axis=0), dd[0:1]
            num0[y, x, kk] = re.astype(BF16)
            num1[x, y, kk] = im.astype(BF16)
            den[pl.ds(kk, 1), :] = dd

        rows = den[...]
        mine = pltpu.roll(rows, (128 - q * SL) % 128, axis=1)
        both = jnp.where(small < SL, mine, pltpu.roll(mine, ROTS, axis=1))
        num0[y, x, OWN] = split(jnp.where(small % ROTS < SL, both, rows[:, ROTS : ROTS + 1]))

    den[...] = jnp.zeros_like(den)

    rb1p, rb1m, rb2p, rb2m = (rb1p0, rb1p1), (rb1m0, rb1m1), (rb2p0, rb2p1), (rb2m0, rb2m1)
    sbp, sbm, rsum, qr = (sbp0, sbp1), (sbm0, sbm1), (rsum0, rsum1), (qr0, qr1)
    outgoing = []

    def go(src, dst, ssem, rsem, dev):
        cp = remote(src, dst, ssem, rsem, dev)
        cp.start()
        outgoing.append(cp)

    def got(dst, ssem, rsem):
        remote(dst, dst, ssem, rsem, (g, c)).wait_recv()

    def axis_dev(h, stage, delta):
        along_y = (h == 0) == (stage == 1)
        return (g, me.at(0, delta) if along_y else me.at(delta, 0))

    lo, hi = slice(0, A_HALF), (slice(A_HALF, SIZE[0]), slice(A_HALF, SIZE[1]))
    nsem = {}

    def sem(h, stage, name):
        key = (h, stage, name)
        if key not in nsem:
            nsem[key] = len(nsem)
        return s1s.at[nsem[key]], s1r.at[nsem[key]]

    def add_high(h, left, right):
        plain = (left[: OWN - A_HALF].astype(F32) + right[: OWN - A_HALF].astype(F32)).astype(BF16)
        if h == 1:
            return plain
        last = split(whole(left[OWN - A_HALF]) + whole(right[OWN - A_HALF]))
        return jnp.concatenate([plain, last[None]], axis=0)

    first = (me.Y, me.X)
    second = (me.X, me.Y)

    def first_sends(h):
        two = num[h].at[(first[h] + 2) % 4]
        go(two.at[:, lo], rb1p[h], *sem(h, 1, "1p"), axis_dev(h, 1, 1))
        go(two.at[:, hi[h]], rb1m[h], *sem(h, 1, "1m"), axis_dev(h, 1, -1))

    def plus_sends(h):
        u = (first[h] + 1) % 4
        go(num[h].at[u, :, hi[h]], rb2p[h].at[:, hi[h]], *sem(h, 1, "2pa"), axis_dev(h, 1, 1))

    def minus_sends(h):
        u = (first[h] + 3) % 4
        go(num[h].at[u, :, lo], rb2m[h].at[:, lo], *sem(h, 1, "2ma"), axis_dev(h, 1, -1))

    def plus_sum(h):
        got(rb1p[h], *sem(h, 1, "1p"))
        for v in range(4):
            sbp[h][v] = (
                num[h][(first[h] + 1) % 4, v, lo].astype(F32) + rb1p[h][v].astype(F32)
            ).astype(BF16)
        go(sbp[h], rb2p[h].at[:, lo], *sem(h, 1, "2pb"), axis_dev(h, 1, 1))

    def minus_sum(h):
        got(rb1m[h], *sem(h, 1, "1m"))
        for v in range(4):
            sbm[h][v] = add_high(h, num[h][(first[h] + 3) % 4, v, hi[h]], rb1m[h][v])
        go(sbm[h], rb2m[h].at[:, hi[h]], *sem(h, 1, "2mb"), axis_dev(h, 1, -1))

    X, Y = me.X, me.Y

    @pl.loop(0, 4)
    def _(n):
        owner_sums((X + 2 + n) % 4, (Y + 2) % 4)

    first_sends(0)

    @pl.loop(0, 3)
    def _(n):
        owner_sums((X + 2) % 4, (Y + 3 + n) % 4)

    first_sends(1)

    @pl.loop(0, 3)
    def _(n):
        owner_sums((X + 3 + n) % 4, (Y + 1) % 4)

    plus_sends(0)
    plus_sum(0)

    @pl.loop(0, 3)
    def _(n):
        owner_sums((X + 3 + n) % 4, (Y + 3) % 4)

    minus_sends(0)
    minus_sum(0)

    @pl.loop(0, 3)
    def _(n):
        owner_sums((X + 3 + n) % 4, Y)

    plus_sends(1)
    minus_sends(1)
    plus_sum(1)
    minus_sum(1)

    for h in (0, 1):
        u, v0 = first[h], second[h]
        got(rb2p[h].at[:, hi[h]], *sem(h, 1, "2pa"))
        got(rb2m[h].at[:, lo], *sem(h, 1, "2ma"))
        got(rb2p[h].at[:, lo], *sem(h, 1, "2pb"))
        got(rb2m[h].at[:, hi[h]], *sem(h, 1, "2mb"))
        for j in (2, 1, 3, 0):
            v = (v0 + j) % 4
            val = (
                num[h][u, v, 0:OWN].astype(F32)
                + rb2p[h][v, 0:OWN].astype(F32)
                + rb2m[h][v, 0:OWN].astype(F32)
            )
            if h == 0:
                tiny = whole(num[h][u, v, OWN]) + whole(rb2p[h][v, OWN]) + whole(rb2m[h][v, OWN])
            if j == 0:
                tf[h * OWN : (h + 1) * OWN] = val
                if h == 0:
                    tf[2 * OWN] = tiny
                continue
            rsum[h][j, 0:OWN] = val.astype(BF16)
            if h == 0:
                rsum[h][j, OWN] = split(tiny)
            go(rsum[h].at[j], qr[h].at[j], *sem(h, 2, str(j)), axis_dev(h, 2, j))
    for h in (0, 1):
        for j in (1, 3, 2):
            got(qr[h].at[j], *sem(h, 2, str(j)))
        tf[h * OWN : (h + 1) * OWN] = (
            tf[h * OWN : (h + 1) * OWN]
            + qr[h][1, 0:OWN].astype(F32)
            + qr[h][2, 0:OWN].astype(F32)
            + qr[h][3, 0:OWN].astype(F32)
        )
    tf[2 * OWN] = tf[2 * OWN] + whole(qr0[1, OWN]) + whole(qr0[2, OWN]) + whole(qr0[3, OWN])
    tf[2 * OWN + 1] = jnp.zeros((SL, FREQ), F32)
    tz[...] = tf[...].astype(BF16)
    tz[2 * OWN] = split(tf[2 * OWN])

    for d in (2, 1, 3):
        peer = (g + 4 * d) % 16
        go(tz.at[pl.ds(peer // 4 * 7, 7)], zr.at[d], zs.at[d], zrs.at[d], (peer, c))
    val = tf[pl.ds(g // 4 * 7, 7)]
    tiny = tf[2 * OWN]
    for d in (1, 3, 2):
        got(zr.at[d], zs.at[d], zrs.at[d])
        val = val + zr[d].astype(F32)
        tiny = tiny + whole(zr[d, 5])
    fall[g, 0:5] = val[0:5].astype(BF16)
    fall[g, 6] = val[6].astype(BF16)
    fall[g, 5] = jnp.where(g // 4 == 3, split(tiny), val[5].astype(BF16))

    for d in (4, 3, 5, 2, 6, 1, 7):
        go(fall.at[g], fall.at[g], fs.at[d], fr.at[d], ((g + 2 * d) % 16, c))
    go(fall.at[g], fall.at[g], ss.at[0], sr.at[0], (sibling, c))
    for d in (1, 7, 2, 6, 3, 5, 4):
        src = fall.at[(g - 2 * d + 16) % 16]
        got(src, fs.at[d], fr.at[d])
        go(src, src, ss.at[d], sr.at[d], (sibling, c))
    for d in range(8):
        src = fall.at[(sibling - 2 * d + 16) % 16]
        got(src, ss.at[d], sr.at[d])
    for cp in sends + group_sends + outgoing:
        cp.wait_send()


def finish_kernel(fall, reg_s, avg_ref, share_ref, wide, *, scale):
    small = [whole(fall[12 + s, 5]) for s in range(GROUP)]
    lane = lax.broadcasted_iota(jnp.int32, (16, 128), 1)
    row = lax.broadcasted_iota(jnp.int32, (16, 128), 0)
    mass = jnp.sum(jnp.where(lane == row, small[0][:, SL : SL + 1], 0.0), axis=0, keepdims=True)
    share_ref[...] = mass[:, :OWN] * scale
    for s in range(GROUP):
        for n in range(4):
            wide[s, pl.ds(n * 7 * SL, 7 * SL), :] = fall[n * 4 + s].astype(F32).reshape(7 * SL, FREQ)
    for s in range(GROUP):
        for r in range(SL):
            shell = s * SL + r
            inverse = 1.0 / (small[s][:OWN, r : r + 1] + reg_s[shell])
            for x in (0, 1):
                rows = wide[s, pl.ds(x * OWN * SL + r, OWN, stride=SL), :]
                first = (x * SHELLS + shell) * FREQ
                avg_ref[:, first : first + FREQ] = rows * inverse


VM = pl.BlockSpec(memory_space=VMEM)
SM = pl.BlockSpec(memory_space=pltpu.SMEM)


def em_sums(particles, references, cand, group_ids, ctf_ids, prior, noise_prec, ctf_turned):
    dma = pltpu.SemaphoreType.DMA
    blk = (SL, FREQ)
    parts = []
    for n in SIZE:
        rest = n - A_HALF
        parts += [
            VMEM((4, 4, n) + blk, BF16),
            VMEM((4, A_HALF) + blk, BF16), VMEM((4, rest) + blk, BF16),
            VMEM((4, n) + blk, BF16), VMEM((4, n) + blk, BF16),
            VMEM((4, A_HALF) + blk, BF16), VMEM((4, rest) + blk, BF16),
            VMEM((4, n) + blk, BF16), VMEM((4, n) + blk, BF16),
        ]
    return pl.pallas_call(
        em_kernel,
        out_shape=(
            jax.ShapeDtypeStruct((16, 7) + blk, BF16),
            jax.ShapeDtypeStruct((1, PART), F32),
        ),
        in_specs=[pl.BlockSpec(memory_space=pl.ANY)] * 2 + [VM, SM, SM, SM, SM] + [VM] * 4,
        out_specs=(VM,) * 2,
        scratch_shapes=[
            VMEM((PART, FEAT), BF16),
            VMEM((OWN, FEAT), BF16),
            VMEM((GROUP, 2, PART * SL, FREQ), F32),
            VMEM((2, OWN * SL, FREQ), F32),
            VMEM((16, 128), jnp.int32),
            VMEM((GROUP, PART, 2, SL, FREQ), BF16),
            VMEM((16, 128), F32),
            VMEM((PART, 128), F32),
            VMEM((GROUP, PART, 2, SL, FREQ), BF16),
            VMEM((GROUP, 64, 2 * ROTS), BF16),
            VMEM((GROUP, CAND, PART), jnp.int32),
            VMEM((GROUP, PART, 128), F32),
            VMEM((GROUP, 16, 128), jnp.int32),
            VMEM((2, K, SL, FREQ), BF16),
            VMEM((256, 128), F32),
            pltpu.SMEM((GROUP, CAND, PART), jnp.int32),
            pltpu.SMEM((GROUP, 16, 128), jnp.int32),
            VMEM((GROUP, 2, 64, 2 * FREQ), F32),
            VMEM((GROUP, 64, 2 * ROTS), F32),
            VMEM((GROUP, 64, 2 * ROTS), F32),
            VMEM((2, 64, 128), F32),
            VMEM((GROUP * PART + 1, 2) + blk, F32),
            VMEM((BLANK + 1, 24, 128), F32),
            VMEM((16, 128), F32),
        ] + parts + [
            VMEM((28,) + blk, F32), VMEM((28,) + blk, BF16), VMEM((4, 7) + blk, BF16),
            dma((N_AG,)), dma((N_AG,)), dma((16,)), dma((16,)),
            dma((4,)), dma((4,)), dma((4,)), dma((4,)),
            dma((4,)), dma((4,)), dma((4,)), dma((4,)),
            dma((4,)), dma((4,)), dma((4,)), dma((4,)), dma((9,)),
            dma((24,)), dma((24,)), dma((4,)), dma((4,)), dma((8,)), dma((8,)), dma((8,)), dma((8,)),
        ],
        compiler_params=pltpu.CompilerParams(collective_id=0, has_side_effects=True),
        name="em",
    )(
        particles, references, cand, cand, group_ids, ctf_ids, prior, noise_prec, ctf_turned,
        jnp.asarray(score_tables()), jnp.asarray(weight_tables()),
    )


def finish(fall, reg, scale):
    return pl.pallas_call(
        functools.partial(finish_kernel, scale=scale),
        out_shape=(
            jax.ShapeDtypeStruct((OWN, FEAT), F32),
            jax.ShapeDtypeStruct((1, OWN), F32),
        ),
        in_specs=[VM, SM],
        out_specs=(VM, VM),
        scratch_shapes=[VMEM((GROUP, 28 * SL, FREQ), F32)],
        name="finish",
    )(fall, reg)


def per_device(
    particles, candidates, group_ids, ctf_ids, ctf_table, noise_prec, references, log_prior, reg
):
    total = PART * lax.axis_size("grp") * lax.axis_size("cls")
    fall, lm = em_sums(
        particles, references, candidates.T, group_ids, ctf_ids, log_prior.astype(F32), noise_prec, ctf_table.T
    )
    averages, share = finish(fall, reg, K / total)
    return (averages, share.reshape(OWN), lm.reshape(PART))


def solution(mesh):
    return jax.shard_map(
        per_device,
        mesh=mesh,
        in_specs=(
            P(("grp", "cls"), None),
            P(("grp", "cls"), None),
            P(("grp", "cls")),
            P(("grp", "cls")),
            P(),
            P(),
            P("cls", None),
            P("cls"),
            P(),
        ),
        out_specs=(P("cls", None), P("cls"), P(("grp", "cls"))),
        check_vma=False,
    )
```

```python
import functools
import math

import jax
import jax.numpy as jnp
import numpy as np
from jax import lax
from jax.experimental import pallas as pl
from jax.experimental.pallas import tpu as pltpu
from jax.sharding import PartitionSpec as P

SHELLS = 64
FREQ = 128
FEAT = 16384
ROTS = 64
K = 208
CAND = 8
OWN = 13
PART = 16
GROUP = 4
SL = SHELLS // GROUP
A_HALF = 7
B_HALF = OWN - A_HALF

MESH = pl.DeviceIdType.MESH
F32 = jnp.float32
BF16 = jnp.bfloat16
HIGH = lax.Precision.HIGHEST
VMEM = pltpu.VMEM


def np_tables():
    turns = np.arange(ROTS)[:, None]
    orders = np.arange(FREQ)[None, :]
    angles = (turns * orders % ROTS) * (2.0 * math.pi / ROTS)
    return np.cos(angles).astype(np.float32), np.sin(angles).astype(np.float32)


def score_tables():
    cos_tab, sin_tab = np_tables()
    both = np.concatenate([cos_tab.T, sin_tab.T], axis=0)
    out = np.zeros((2, 2 * FREQ, 2 * ROTS), np.float32)
    out[0, :, :ROTS] = both
    out[1, :, ROTS:] = both
    return out


def weight_tables():
    cos_tab, sin_tab = np_tables()
    both = np.concatenate([cos_tab, sin_tab], axis=1)
    out = np.zeros((2, 2 * ROTS, 2 * FREQ), np.float32)
    out[0, :ROTS] = both
    out[1, ROTS:] = both
    return out


def remote(src, dst, ssem, rsem, device):
    return pltpu.make_async_remote_copy(
        src_ref=src, dst_ref=dst, send_sem=ssem, recv_sem=rsem, device_id=device, device_id_type=MESH
    )


def split(value):
    high = value.astype(BF16)
    left = lax.broadcasted_iota(jnp.int32, value.shape, len(value.shape) - 1) < ROTS
    return jnp.where(left, high.astype(F32), value - high.astype(F32)).astype(BF16)


def whole(pair):
    wide = pair.astype(F32)
    return wide + pltpu.roll(wide, ROTS, axis=1)


class Plane:
    def __init__(self):
        self.g = lax.axis_index("grp")
        self.c = lax.axis_index("cls")
        self.X = self.c // 4
        self.Y = self.c % 4

    def at(self, dx, dy):
        return ((self.X + dx) % 4) * 4 + (self.Y + dy) % 4


N_AG = 40


SIZE = (OWN + 1, OWN)
BLANK = GROUP * PART * CAND


def em_kernel(
    part_hbm, refs_hbm, cand_ref, cand_sm, gid_sm, cid_sm, prior_ref, noise_ref, ctf_ref, tab_ref, wtab_ref,
    fall, lm_ref,
    part_ref, own_ref, spread, spread_refs, slot_ref, w4_ref, pwb_ref, side_ref,
    wall, wt_all, cand_all, side_all, slot_all,
    refs_all, pw_all, cand_s, slot_s, acc, sc_send, sc_recv, gmat,
    wf, fac, den,
    num0, rb1p0, rb1m0, rb2p0, rb2m0, sbp0, sbm0, rsum0, qr0,
    num1, rb1p1, rb1m1, rb2p1, rb2m1, sbp1, sbm1, rsum1, qr1,
    tf, tz, zr,
    ag_send, ag_recv, pw_send, pw_recv, gw_send, gw_recv, gc_send, gc_recv,
    gs_send, gs_recv, gt_send, gt_recv, gd_send, gd_recv, gl_send, gl_recv, loc_sem,
    s1s, s1r, zs, zrs, fs, fr, ss, sr,
):
    me = Plane()
    g, c = me.g, me.c
    q = g % GROUP
    base = g - q

    def member(d):
        return base + (q + d) % GROUP

    sibling = g // 2 * 2 + (g + 1) % 2
    barrier = pltpu.get_barrier_semaphore()
    for d in range(1, 16):
        pl.semaphore_signal(barrier, inc=1, device_id=(g, (c + d) % 16), device_id_type=MESH)
        pl.semaphore_signal(barrier, inc=1, device_id=((g + d) % 16, c), device_id_type=MESH)
    load_refs = pltpu.make_async_copy(refs_hbm, own_ref, loc_sem.at[3])
    load_refs.start()
    load_part = pltpu.make_async_copy(part_hbm, part_ref, loc_sem.at[4])
    load_part.start()

    lane16 = lax.broadcasted_iota(jnp.int32, (16, 128), 1)
    row16 = lax.broadcasted_iota(jnp.int32, (16, 128), 0)

    place = jnp.where(lane16 < 2 * OWN, row16 * (2 * OWN) + lane16, -1)
    last = jnp.full((16, 128), BLANK, jnp.int32)
    head = jnp.full((16, 128), BLANK, jnp.int32)
    for n in range(PART * CAND):
        low = place == 2 * cand_sm[n % CAND, n // CAND]
        last = jnp.where(low, q * (PART * CAND) + n, last)
        m = PART * CAND - 1 - n
        high = place == 2 * cand_sm[m % CAND, m // CAND]
        head = jnp.where(high, q * (PART * CAND) + m, head)
    other = jnp.where(head == last, BLANK, head)
    slot_ref[...] = jnp.where(lane16 % 2 == 0, last, pltpu.roll(other, 1, axis=1))

    def picked(ids, table, rows_are_lanes):
        count = table.shape[1] if rows_are_lanes else table.shape[0]
        spot = lax.broadcasted_iota(jnp.int32, (PART, count), 1)
        which = lax.broadcasted_iota(jnp.int32, (PART, count), 0)
        wanted = jnp.zeros((PART, count), jnp.int32)
        for i in range(PART):
            wanted = jnp.where(which == i, ids[i], wanted)
        hot = (wanted == spot).astype(F32).astype(BF16)
        dims = (((1,), (1 if rows_are_lanes else 0,)), ((), ()))
        rest, rows = table, jnp.zeros((PART, SHELLS), F32)
        for _ in range(3):
            piece = rest.astype(BF16)
            rest = rest - piece.astype(F32)
            rows = rows + lax.dot_general(hot, piece, dims, preferred_element_type=F32)
        return rows

    precision_rows = picked(gid_sm, noise_ref[...], False)
    ctf_rows = picked(cid_sm, ctf_ref[...], True)
    shell_weight = precision_rows * ctf_rows
    side_ref[:, SHELLS:] = jnp.ones((PART, 128 - SHELLS), F32)
    side_ref[:, :SHELLS] = (shell_weight * ctf_rows).astype(BF16).astype(F32)

    load_refs.wait()
    for x in (0, 1):
        for r in range(SL):
            first = pl.multiple_of((x * SHELLS + q * SL + r) * FREQ, FREQ)
            spread_refs[x, pl.ds(r, OWN, stride=SL), :] = own_ref[:, pl.ds(first, FREQ)].astype(F32)
        refs_all[x, pl.ds(c * OWN, OWN)] = (
            spread_refs[x].reshape(OWN, SL, FREQ).astype(BF16)
        )
    table = jnp.zeros((OWN, 128), F32)
    lane13 = lax.broadcasted_iota(jnp.int32, (OWN, 128), 1)
    for r in range(SHELLS):
        re = own_ref[:, r * FREQ : (r + 1) * FREQ].astype(F32)
        im = own_ref[:, (SHELLS + r) * FREQ : (SHELLS + r + 1) * FREQ].astype(F32)
        power = jnp.sum(re * re + im * im, axis=1, keepdims=True)
        table = jnp.where(lane13 == r, -0.5 * power, table)
    prior = jnp.broadcast_to(prior_ref[...].astype(F32).reshape(1, OWN), (OWN, OWN))
    square = lax.broadcasted_iota(jnp.int32, (OWN, OWN), 0) == lax.broadcasted_iota(jnp.int32, (OWN, OWN), 1)
    column = jnp.sum(jnp.where(square, prior, 0.0), axis=1, keepdims=True)
    table = jnp.where(lane13 == SHELLS, column, table)
    pwb_ref[...] = jnp.zeros((16, 128), F32)
    pwb_ref[0:OWN] = table

    load_part.wait()
    for s in range(GROUP):
        for r in range(SL):
            shell = s * SL + r
            column = shell_weight[:, shell : shell + 1]
            for x in (0, 1):
                first = (x * SHELLS + shell) * FREQ
                spread[s, x, pl.ds(r, PART, stride=SL), :] = (
                    part_ref[:, first : first + FREQ].astype(F32) * column
                )
        for x in (0, 1):
            w4_ref[s, :, x] = spread[s, x].reshape(PART, SL, FREQ).astype(BF16)

    pl.semaphore_wait(barrier, 30)

    def offs(h, i, j):
        return me.at(i, j) if h == 0 else me.at(j, i)

    def block(h, i, j, part):
        first = offs(h, i, j) * OWN
        if part == 0:
            return refs_all.at[h, pl.ds(first, OWN)]
        if part == 1:
            return refs_all.at[h, pl.ds(first, A_HALF)]
        return refs_all.at[h, pl.ds(first + A_HALF, B_HALF)]

    sends = []

    def send(m, src, dst, dev):
        cp = remote(src, dst, ag_send.at[m], ag_recv.at[m], (g, dev))
        cp.start()
        sends.append(cp)

    def arrived(m, dst):
        remote(dst, dst, ag_send.at[m], ag_recv.at[m], (g, c)).wait_recv()

    mine = [block(h, 0, 0, 0) for h in (0, 1)]
    where = (0, -1, 1, 2)

    def stage_two(h, n):
        i = where[n]
        src = mine[h] if n == 0 else block(h, i, 0, 0)
        m = h * 20 + 4 + 4 * n
        send(m, src, block(h, i, 0, 0), offs(h, 0, 1))
        send(m + 1, src, block(h, i, 0, 0), offs(h, 0, -1))

    def forward_two(h, n):
        i = where[n]
        m = h * 20 + 4 + 4 * n
        arrived(m, block(h, i, -1, 0))
        send(m + 2, block(h, i, -1, 1), block(h, i, -1, 1), offs(h, 0, 1))
        arrived(m + 1, block(h, i, 1, 0))
        send(m + 3, block(h, i, 1, 2), block(h, i, 1, 2), offs(h, 0, -1))

    for h in (0, 1):
        send(h * 20 + 0, mine[h], block(h, 0, 0, 0), offs(h, 1, 0))
        send(h * 20 + 1, mine[h], block(h, 0, 0, 0), offs(h, -1, 0))
    for h in (0, 1):
        stage_two(h, 0)

    group_sends = []
    for d in range(1, GROUP):
        cp = remote(cand_ref, cand_all.at[q], gc_send.at[d], gc_recv.at[d], (member(d), c))
        cp.start()
        group_sends.append(cp)
        cp = remote(slot_ref, slot_all.at[q], gl_send.at[d], gl_recv.at[d], (member(d), c))
        cp.start()
        group_sends.append(cp)
        cp = remote(side_ref, side_all.at[q], gd_send.at[d], gd_recv.at[d], (member(d), c))
        cp.start()
        group_sends.append(cp)
        cp = remote(
            w4_ref.at[(q + d) % GROUP], wall.at[q], gw_send.at[d], gw_recv.at[d], (member(d), c)
        )
        cp.start()
        group_sends.append(cp)
    row0 = pl.multiple_of(c * 16, 16)
    for d in range(1, 16):
        cp = remote(
            pwb_ref, pw_all.at[pl.ds(row0, 16)], pw_send.at[d], pw_recv.at[d], (g, (c + d) % 16)
        )
        cp.start()
        group_sends.append(cp)
    local = [
        pltpu.make_async_copy(w4_ref.at[q], wall.at[q], loc_sem.at[0]),
        pltpu.make_async_copy(cand_ref, cand_all.at[q], loc_sem.at[1]),
        pltpu.make_async_copy(pwb_ref, pw_all.at[pl.ds(row0, 16)], loc_sem.at[2]),
        pltpu.make_async_copy(side_ref, side_all.at[q], loc_sem.at[6]),
        pltpu.make_async_copy(slot_ref, slot_all.at[q], loc_sem.at[7]),
    ]
    for cp in local:
        cp.start()

    for h in (0, 1):
        m = h * 20
        arrived(m, block(h, -1, 0, 0))
        send(m + 2, block(h, -1, 0, 1), block(h, -1, 0, 1), offs(h, 1, 0))
        stage_two(h, 1)
        arrived(m + 1, block(h, 1, 0, 0))
        send(m + 3, block(h, 1, 0, 2), block(h, 1, 0, 2), offs(h, -1, 0))
        stage_two(h, 2)
    for h in (0, 1):
        forward_two(h, 0)
    for h in (0, 1):
        arrived(h * 20 + 2, block(h, 2, 0, 1))
        arrived(h * 20 + 3, block(h, 2, 0, 2))
        stage_two(h, 3)
    for n in (1, 2, 3):
        for h in (0, 1):
            forward_two(h, n)

    for cp in local:
        cp.wait()
    for d in range(1, 16):
        rows = pw_all.at[pl.ds(pl.multiple_of((c - d + 16) % 16 * 16, 16), 16)]
        remote(rows, rows, pw_send.at[d], pw_recv.at[d], (g, c)).wait_recv()
    for d in range(1, GROUP):
        slot = cand_all.at[(q - d + GROUP) % GROUP]
        remote(slot, slot, gc_send.at[d], gc_recv.at[d], (g, c)).wait_recv()
    for d in range(1, GROUP):
        slot = slot_all.at[(q - d + GROUP) % GROUP]
        remote(slot, slot, gl_send.at[d], gl_recv.at[d], (g, c)).wait_recv()
    to_smem = pltpu.make_async_copy(cand_all, cand_s, loc_sem.at[5])
    to_smem.start()
    slots_to_smem = pltpu.make_async_copy(slot_all, slot_s, loc_sem.at[8])
    slots_to_smem.start()
    for i in range(PART):
        side_row = side_ref[i : i + 1, :]
        for t in range(CAND):
            k = cand_sm[t, i]
            gmat[i // 8, (i % 8) * 8 + t : (i % 8) * 8 + t + 1, :] = (
                side_row * pw_all[pl.ds(k // OWN * 16 + k % OWN, 1), :]
            )
    to_smem.wait()
    slots_to_smem.wait()
    for d in range(1, GROUP):
        slot = side_all.at[(q - d + GROUP) % GROUP]
        remote(slot, slot, gd_send.at[d], gd_recv.at[d], (g, c)).wait_recv()
        slot = wall.at[(q - d + GROUP) % GROUP]
        remote(slot, slot, gw_send.at[d], gw_recv.at[d], (g, c)).wait_recv()

    @pl.loop(0, GROUP * PART)
    def _(n):
        wf[n] = wall[n // PART, n % PART].astype(F32)

    wf[GROUP * PART] = jnp.zeros((2, SL, FREQ), F32)
    for h in (0, 1):
        for n in range(4):
            m = h * 20 + 4 + 4 * n
            arrived(m + 2, block(h, where[n], 2, 1))
            arrived(m + 3, block(h, where[n], 2, 2))

    @pl.loop(0, GROUP * PART)
    def _(n):
        s, i = n // PART, n % PART
        w_re, w_im = wf[n, 0], wf[n, 1]
        inner, outer = [], []
        for t in range(CAND):
            k = cand_s[s, t, i]
            a_re = refs_all[0, k].astype(F32)
            a_im = refs_all[1, k].astype(F32)
            one = w_re * a_re + w_im * a_im
            two = w_re * a_im - w_im * a_re
            inner.append(jnp.sum(one, axis=0, keepdims=True))
            outer.append(jnp.sum(two, axis=0, keepdims=True))
        rows = pl.ds(pl.multiple_of(i % 8 * 8, 8), 8)
        acc[s, i // 8, rows, 0:FREQ] = jnp.concatenate(inner, axis=0)
        acc[s, i // 8, rows, FREQ : 2 * FREQ] = jnp.concatenate(outer, axis=0)

    @pl.loop(0, GROUP)
    def _(s):
        sc_send[s] = jnp.dot(
            acc[s, 0], tab_ref[0], precision=HIGH, preferred_element_type=F32
        ) + jnp.dot(acc[s, 1], tab_ref[1], precision=HIGH, preferred_element_type=F32)

    for d in range(1, GROUP):
        cp = remote(
            sc_send.at[(q + d) % GROUP], sc_recv.at[d], gs_send.at[d], gs_recv.at[d], (member(d), c)
        )
        cp.start()
        group_sends.append(cp)
    sc = sc_send[q]
    wide = lax.broadcasted_iota(jnp.int32, (64, 2 * ROTS), 1) < ROTS
    sc = sc + jnp.where(
        wide,
        jnp.sum(gmat[0], axis=1, keepdims=True),
        jnp.sum(gmat[1], axis=1, keepdims=True),
    )
    for d in range(1, GROUP):
        remote(sc_recv.at[d], sc_recv.at[d], gs_send.at[d], gs_recv.at[d], (g, c)).wait_recv()
    sc = sc + sc_recv[1] + sc_recv[2] + sc_recv[3]

    sc = sc.reshape(8, 8, 2 * ROTS)
    left = lax.broadcasted_iota(jnp.int32, (8, 2 * ROTS), 1) < ROTS
    low = jnp.max(sc, axis=1)
    best_l = jnp.max(jnp.where(left, low, -jnp.inf), axis=1, keepdims=True)
    best_r = jnp.max(jnp.where(left, -jnp.inf, low), axis=1, keepdims=True)
    best = jnp.where(left, best_l, best_r)
    expo = jnp.exp(sc - best[:, None, :])
    part = jnp.sum(expo, axis=1)
    tot_l = jnp.sum(jnp.where(left, part, 0.0), axis=1, keepdims=True)
    tot_r = jnp.sum(jnp.where(left, 0.0, part), axis=1, keepdims=True)
    total = jnp.where(left, tot_l, tot_r)
    spot = lax.broadcasted_iota(jnp.int32, (8, 2 * ROTS), 1)
    particle = lax.broadcasted_iota(jnp.int32, (8, 2 * ROTS), 0)
    mass = jnp.where(spot == particle, tot_l, jnp.where(spot == particle + 8, tot_r, 0.0))
    lm_ref[...] = jnp.log(jnp.sum(mass, axis=0, keepdims=True)[:, :PART])
    wt_all[q] = (expo / total[:, None, :]).reshape(64, 2 * ROTS).astype(BF16)
    for d in range(1, GROUP):
        cp = remote(
            wt_all.at[q], wt_all.at[q], gt_send.at[d], gt_recv.at[d], (member(d), c)
        )
        cp.start()
        group_sends.append(cp)
    for d in range(1, GROUP):
        slot = wt_all.at[(q - d + GROUP) % GROUP]
        remote(slot, slot, gt_send.at[d], gt_recv.at[d], (g, c)).wait_recv()

    lane = lax.broadcasted_iota(jnp.int32, (64, 128), 1)
    for s in range(GROUP):
        wt = wt_all[s].astype(F32)
        for half in (0, 1):
            rows = jnp.dot(wt, wtab_ref[half], precision=HIGH, preferred_element_type=F32)
            rows = rows.astype(BF16).astype(F32)
            first = s * PART * CAND + half * 64
            for n in range(64):
                fac[first + n, 0:8] = jnp.broadcast_to(rows[n : n + 1, :FREQ], (8, FREQ))
                fac[first + n, 8:16] = jnp.broadcast_to(rows[n : n + 1, FREQ:], (8, FREQ))
            part = jnp.where((lane < ROTS) == (half == 0), wt, 0.0)
            mass = jnp.sum(part, axis=1, keepdims=True)
            for i in range(8):
                terms = mass[i * 8 : i * 8 + 8] * side_all[s, half * 8 + i : half * 8 + i + 1, :]
                for t in range(CAND):
                    fac[first + i * 8 + t, 16:24] = jnp.broadcast_to(terms[t : t + 1], (8, 128))
    fac[BLANK] = jnp.zeros((24, 128), F32)

    num = (num0, num1)
    small = lax.broadcasted_iota(jnp.int32, (16, 128), 1)

    def owner_sums(x, y):
        o = x * 4 + y

        @pl.loop(0, OWN)
        def _(kk):
            re = [jnp.zeros((8, FREQ), F32)] * 2
            im = [jnp.zeros((8, FREQ), F32)] * 2
            dd = jnp.zeros((8, 128), F32)
            for s in range(GROUP):
                for m in range(2):
                    row = slot_s[s, o, kk * 2 + m]
                    p = row >> 3
                    wc, ws = fac[row, 0:8], fac[row, 8:16]
                    for n in (0, 1):
                        w_re, w_im = wf[p, 0, n * 8 : n * 8 + 8], wf[p, 1, n * 8 : n * 8 + 8]
                        re[n] = re[n] + (w_re * wc - w_im * ws)
                        im[n] = im[n] + (w_re * ws + w_im * wc)
                    dd = dd + fac[row, 16:24]
            re, im, dd = jnp.concatenate(re, axis=0), jnp.concatenate(im, axis=0), dd[0:1]
            num0[y, x, kk] = re.astype(BF16)
            num1[x, y, kk] = im.astype(BF16)
            den[pl.ds(kk, 1), :] = dd

        rows = den[...]
        mine = pltpu.roll(rows, (128 - q * SL) % 128, axis=1)
        both = jnp.where(small < SL, mine, pltpu.roll(mine, ROTS, axis=1))
        num0[y, x, OWN] = split(jnp.where(small % ROTS < SL, both, rows[:, ROTS : ROTS + 1]))

    den[...] = jnp.zeros_like(den)

    rb1p, rb1m, rb2p, rb2m = (rb1p0, rb1p1), (rb1m0, rb1m1), (rb2p0, rb2p1), (rb2m0, rb2m1)
    sbp, sbm, rsum, qr = (sbp0, sbp1), (sbm0, sbm1), (rsum0, rsum1), (qr0, qr1)
    outgoing = []

    def go(src, dst, ssem, rsem, dev):
        cp = remote(src, dst, ssem, rsem, dev)
        cp.start()
        outgoing.append(cp)

    def got(dst, ssem, rsem):
        remote(dst, dst, ssem, rsem, (g, c)).wait_recv()

    def axis_dev(h, stage, delta):
        along_y = (h == 0) == (stage == 1)
        return (g, me.at(0, delta) if along_y else me.at(delta, 0))

    lo, hi = slice(0, A_HALF), (slice(A_HALF, SIZE[0]), slice(A_HALF, SIZE[1]))
    nsem = {}

    def sem(h, stage, name):
        key = (h, stage, name)
        if key not in nsem:
            nsem[key] = len(nsem)
        return s1s.at[nsem[key]], s1r.at[nsem[key]]

    def add_high(h, left, right):
        plain = (left[: OWN - A_HALF].astype(F32) + right[: OWN - A_HALF].astype(F32)).astype(BF16)
        if h == 1:
            return plain
        last = split(whole(left[OWN - A_HALF]) + whole(right[OWN - A_HALF]))
        return jnp.concatenate([plain, last[None]], axis=0)

    first = (me.Y, me.X)
    second = (me.X, me.Y)

    LATE = (2, 3, 1, 0)

    def first_send(h, j):
        v = (second[h] + j) % 4
        two = num[h].at[(first[h] + 2) % 4, v]
        go(two.at[lo], rb1p[h].at[v], *sem(h, 1, f"1p{j}"), axis_dev(h, 1, 1))
        go(two.at[hi[h]], rb1m[h].at[v], *sem(h, 1, f"1m{j}"), axis_dev(h, 1, -1))

    def plus_sends(h):
        u = (first[h] + 1) % 4
        go(num[h].at[u, :, hi[h]], rb2p[h].at[:, hi[h]], *sem(h, 1, "2pa"), axis_dev(h, 1, 1))

    def minus_sends(h):
        u = (first[h] + 3) % 4
        go(num[h].at[u, :, lo], rb2m[h].at[:, lo], *sem(h, 1, "2ma"), axis_dev(h, 1, -1))

    def plus_sum(h, j):
        v = (second[h] + j) % 4
        got(rb1p[h].at[v], *sem(h, 1, f"1p{j}"))
        sbp[h][v] = (
            num[h][(first[h] + 1) % 4, v, lo].astype(F32) + rb1p[h][v].astype(F32)
        ).astype(BF16)
        go(sbp[h].at[v], rb2p[h].at[v, lo], *sem(h, 1, f"2pb{j}"), axis_dev(h, 1, 1))

    def minus_sum(h, j):
        v = (second[h] + j) % 4
        got(rb1m[h].at[v], *sem(h, 1, f"1m{j}"))
        sbm[h][v] = add_high(h, num[h][(first[h] + 3) % 4, v, hi[h]], rb1m[h][v])
        go(sbm[h].at[v], rb2m[h].at[v, hi[h]], *sem(h, 1, f"2mb{j}"), axis_dev(h, 1, -1))

    X, Y = me.X, me.Y
    for j in LATE:
        owner_sums((X + j) % 4, (Y + 2) % 4)
        first_send(0, j)
        if j == 2:
            first_send(1, 2)
    for j in LATE[1:]:
        owner_sums((X + 2) % 4, (Y + j) % 4)
        first_send(1, j)

    @pl.loop(0, 3)
    def _(n):
        owner_sums((X + 3 + n) % 4, (Y + 1) % 4)

    plus_sends(0)
    for j in LATE:
        plus_sum(0, j)

    @pl.loop(0, 3)
    def _(n):
        owner_sums((X + 3 + n) % 4, (Y + 3) % 4)

    minus_sends(0)
    for j in LATE:
        minus_sum(0, j)

    @pl.loop(0, 3)
    def _(n):
        owner_sums((X + 3 + n) % 4, Y)

    plus_sends(1)
    minus_sends(1)
    for j in LATE:
        plus_sum(1, j)
        minus_sum(1, j)

    for h in (0, 1):
        u, v0 = first[h], second[h]
        got(rb2p[h].at[:, hi[h]], *sem(h, 1, "2pa"))
        got(rb2m[h].at[:, lo], *sem(h, 1, "2ma"))
        for j in LATE:
            v = (v0 + j) % 4
            got(rb2p[h].at[v, lo], *sem(h, 1, f"2pb{j}"))
            got(rb2m[h].at[v, hi[h]], *sem(h, 1, f"2mb{j}"))
            val = (
                num[h][u, v, 0:OWN].astype(F32)
                + rb2p[h][v, 0:OWN].astype(F32)
                + rb2m[h][v, 0:OWN].astype(F32)
            )
            if h == 0:
                tiny = whole(num[h][u, v, OWN]) + whole(rb2p[h][v, OWN]) + whole(rb2m[h][v, OWN])
            if j == 0:
                tf[h * OWN : (h + 1) * OWN] = val
                if h == 0:
                    tf[2 * OWN] = tiny
                continue
            rsum[h][j, 0:OWN] = val.astype(BF16)
            if h == 0:
                rsum[h][j, OWN] = split(tiny)
            go(rsum[h].at[j], qr[h].at[j], *sem(h, 2, str(j)), axis_dev(h, 2, j))
    for h in (0, 1):
        for j in (1, 3, 2):
            got(qr[h].at[j], *sem(h, 2, str(j)))
        tf[h * OWN : (h + 1) * OWN] = (
            tf[h * OWN : (h + 1) * OWN]
            + qr[h][1, 0:OWN].astype(F32)
            + qr[h][2, 0:OWN].astype(F32)
            + qr[h][3, 0:OWN].astype(F32)
        )
    tf[2 * OWN] = tf[2 * OWN] + whole(qr0[1, OWN]) + whole(qr0[2, OWN]) + whole(qr0[3, OWN])
    tf[2 * OWN + 1] = jnp.zeros((SL, FREQ), F32)
    tz[...] = tf[...].astype(BF16)
    tz[2 * OWN] = split(tf[2 * OWN])

    for d in (2, 1, 3):
        peer = (g + 4 * d) % 16
        go(tz.at[pl.ds(peer // 4 * 7, 7)], zr.at[d], zs.at[d], zrs.at[d], (peer, c))
    val = tf[pl.ds(g // 4 * 7, 7)]
    tiny = tf[2 * OWN]
    for d in (1, 3, 2):
        got(zr.at[d], zs.at[d], zrs.at[d])
        val = val + zr[d].astype(F32)
        tiny = tiny + whole(zr[d, 5])
    fall[g, 0:5] = val[0:5].astype(BF16)
    fall[g, 6] = val[6].astype(BF16)
    fall[g, 5] = jnp.where(g // 4 == 3, split(tiny), val[5].astype(BF16))

    for d in (4, 3, 5, 2, 6, 1, 7):
        go(fall.at[g], fall.at[g], fs.at[d], fr.at[d], ((g + 2 * d) % 16, c))
    go(fall.at[g], fall.at[g], ss.at[0], sr.at[0], (sibling, c))
    for d in (1, 7, 2, 6, 3, 5, 4):
        src = fall.at[(g - 2 * d + 16) % 16]
        got(src, fs.at[d], fr.at[d])
        go(src, src, ss.at[d], sr.at[d], (sibling, c))
    for d in range(8):
        src = fall.at[(sibling - 2 * d + 16) % 16]
        got(src, ss.at[d], sr.at[d])
    for cp in sends + group_sends + outgoing:
        cp.wait_send()


def finish_kernel(fall, lm_in, reg_s, avg_ref, share_ref, lm_ref, wide, *, scale):
    lm_ref[...] = lm_in[0, :]
    small = [whole(fall[12 + s, 5]) for s in range(GROUP)]
    lane = lax.broadcasted_iota(jnp.int32, (16, 128), 1)
    row = lax.broadcasted_iota(jnp.int32, (16, 128), 0)
    mass = jnp.sum(jnp.where(lane == row, small[0][:, SL : SL + 1], 0.0), axis=0, keepdims=True)
    share_ref[...] = mass[0, :OWN] * scale
    for s in range(GROUP):
        for n in range(4):
            wide[s, pl.ds(n * 7 * SL, 7 * SL), :] = fall[n * 4 + s].astype(F32).reshape(7 * SL, FREQ)
    for s in range(GROUP):
        for r in range(SL):
            shell = s * SL + r
            inverse = 1.0 / (small[s][:OWN, r : r + 1] + reg_s[shell])
            for x in (0, 1):
                rows = wide[s, pl.ds(x * OWN * SL + r, OWN, stride=SL), :]
                first = (x * SHELLS + shell) * FREQ
                avg_ref[:, first : first + FREQ] = rows * inverse


VM = pl.BlockSpec(memory_space=VMEM)
SM = pl.BlockSpec(memory_space=pltpu.SMEM)


def em_sums(particles, references, cand, group_ids, ctf_ids, prior, noise_prec, ctf_turned):
    dma = pltpu.SemaphoreType.DMA
    blk = (SL, FREQ)
    parts = []
    for n in SIZE:
        rest = n - A_HALF
        parts += [
            VMEM((4, 4, n) + blk, BF16),
            VMEM((4, A_HALF) + blk, BF16), VMEM((4, rest) + blk, BF16),
            VMEM((4, n) + blk, BF16), VMEM((4, n) + blk, BF16),
            VMEM((4, A_HALF) + blk, BF16), VMEM((4, rest) + blk, BF16),
            VMEM((4, n) + blk, BF16), VMEM((4, n) + blk, BF16),
        ]
    return pl.pallas_call(
        em_kernel,
        out_shape=(
            jax.ShapeDtypeStruct((16, 7) + blk, BF16),
            jax.ShapeDtypeStruct((1, PART), F32),
        ),
        in_specs=[pl.BlockSpec(memory_space=pl.ANY)] * 2 + [VM, SM, SM, SM] + [VM] * 5,
        out_specs=(VM,) * 2,
        scratch_shapes=[
            VMEM((PART, FEAT), BF16),
            VMEM((OWN, FEAT), BF16),
            VMEM((GROUP, 2, PART * SL, FREQ), F32),
            VMEM((2, OWN * SL, FREQ), F32),
            VMEM((16, 128), jnp.int32),
            VMEM((GROUP, PART, 2, SL, FREQ), BF16),
            VMEM((16, 128), F32),
            VMEM((PART, 128), F32),
            VMEM((GROUP, PART, 2, SL, FREQ), BF16),
            VMEM((GROUP, 64, 2 * ROTS), BF16),
            VMEM((GROUP, CAND, PART), jnp.int32),
            VMEM((GROUP, PART, 128), F32),
            VMEM((GROUP, 16, 128), jnp.int32),
            VMEM((2, K, SL, FREQ), BF16),
            VMEM((256, 128), F32),
            pltpu.SMEM((GROUP, CAND, PART), jnp.int32),
            pltpu.SMEM((GROUP, 16, 128), jnp.int32),
            VMEM((GROUP, 2, 64, 2 * FREQ), F32),
            VMEM((GROUP, 64, 2 * ROTS), F32),
            VMEM((GROUP, 64, 2 * ROTS), F32),
            VMEM((2, 64, 128), F32),
            VMEM((GROUP * PART + 1, 2) + blk, F32),
            VMEM((BLANK + 1, 24, 128), F32),
            VMEM((16, 128), F32),
        ] + parts + [
            VMEM((28,) + blk, F32), VMEM((28,) + blk, BF16), VMEM((4, 7) + blk, BF16),
            dma((N_AG,)), dma((N_AG,)), dma((16,)), dma((16,)),
            dma((4,)), dma((4,)), dma((4,)), dma((4,)),
            dma((4,)), dma((4,)), dma((4,)), dma((4,)),
            dma((4,)), dma((4,)), dma((4,)), dma((4,)), dma((9,)),
            dma((44,)), dma((44,)), dma((4,)), dma((4,)), dma((8,)), dma((8,)), dma((8,)), dma((8,)),
        ],
        compiler_params=pltpu.CompilerParams(collective_id=0, has_side_effects=True),
        name="em",
    )(
        particles, references, cand, cand, group_ids, ctf_ids, prior, noise_prec, ctf_turned,
        jnp.asarray(score_tables()), jnp.asarray(weight_tables()),
    )


def finish(fall, lm, reg, scale):
    return pl.pallas_call(
        functools.partial(finish_kernel, scale=scale),
        out_shape=(
            jax.ShapeDtypeStruct((OWN, FEAT), F32),
            jax.ShapeDtypeStruct((OWN,), F32),
            jax.ShapeDtypeStruct((PART,), F32),
        ),
        in_specs=[VM, VM, SM],
        out_specs=(VM, VM, VM),
        scratch_shapes=[VMEM((GROUP, 28 * SL, FREQ), F32)],
        name="finish",
    )(fall, lm, reg)


def per_device(
    particles, candidates, group_ids, ctf_ids, ctf_table, noise_prec, references, log_prior, reg
):
    total = PART * lax.axis_size("grp") * lax.axis_size("cls")
    fall, lm = em_sums(
        particles, references, candidates.T, group_ids, ctf_ids, log_prior, noise_prec, ctf_table.T
    )
    return finish(fall, lm, reg, K / total)


def solution(mesh):
    return jax.shard_map(
        per_device,
        mesh=mesh,
        in_specs=(
            P(("grp", "cls"), None),
            P(("grp", "cls"), None),
            P(("grp", "cls")),
            P(("grp", "cls")),
            P(),
            P(),
            P("cls", None),
            P("cls"),
            P(),
        ),
        out_specs=(P("cls", None), P("cls"), P(("grp", "cls"))),
        check_vma=False,
    )
```
